256 devices in a mesh: chan: 64 (over z_hi, x, y, core), tm: 4 (over z_lo).
Axes of the slice: x: 4, y: 4, z: 8 (z_hi: 2, z_lo: 4; z = z_hi * 4 + z_lo), core: 2. Of those that a mesh axis runs over, the one named last changes fastest.
Arguments:
- spectra: bfloat16 [64, 8, 2, 6144], P(None, 'tm', None, 'chan'), may hold values from -120 to 120
- bad_channels: int32 [6144], P('chan'), may hold values 0 or 1
- tile_list: int32 [512, 2], P('chan'), may hold values from 0 to 47, as said below
Outputs:
- correlations: float32 [512, 32, 128, 128], P(('chan', 'tm'))
The draws below stay inside these ranges and needn't reach their ends.
Inputs may be any that keep to these rules, and one draw needn't show every extreme that they name: `tile_list`: each row (a, b) has a <= b; a pair may appear more than once.
All inputs are finite; a program needn't handle non-finite values. No bound on the sum of `bad_channels` on one device may be relied on, other than what follows from the above.
Results may differ from the reference program's by a relative error of at most 0.004.
Values may be sent and summed in bfloat16 or wider, within the bound.
A program may use at most 128 MiB of HBM per device.

```python
import math
import jax
import jax.numpy as jnp
from jax import lax

F = 64
LAGS = 32
TILE = 128
CHANNELS = 6144
HOURS = 8
TILES = 512


def draw_spectra(key, part):
    key_base, key_bins, key_chan = jax.random.split(key, 3)
    full_shape = (F, HOURS, 2, CHANNELS)
    noise_base = jnp.clip(jax.random.normal(key_base, full_shape, jnp.float32), -4.0, 4.0)
    bin_scale = jnp.exp(jax.random.uniform(key_bins, (F, 1, 1, CHANNELS), jnp.float32, 0.0, math.log(10.0)))
    chan_scale = jnp.exp(jax.random.uniform(key_chan, (1, HOURS, 1, CHANNELS), jnp.float32, math.log(0.3), math.log(3.0)))
    return (noise_base * bin_scale * chan_scale).astype(jnp.bfloat16)


def draw_tile_list(key, part):
    block_total = CHANNELS // TILE
    key_one, key_two = jax.random.split(key, 2)
    pick_one = jax.random.randint(key_one, (TILES,), 0, block_total)
    pick_two = jax.random.randint(key_two, (TILES,), 0, block_total)
    lower_idx = jnp.minimum(pick_one, pick_two)
    upper_idx = jnp.maximum(pick_one, pick_two)
    upper_idx = upper_idx.at[0].set(block_total - 1)
    lower_idx = lower_idx.at[1].set(0)
    return jnp.stack([lower_idx, upper_idx], axis=1).astype(jnp.int32)


def with_ends(drawn, rng, least, largest):
    longest = drawn.shape.index(max(drawn.shape))
    spots = []
    for shift in (0, 1):
        where = [jax.random.randint(jax.random.fold_in(rng, axis), (), 0, length) for axis, length in enumerate(drawn.shape)]
        where[longest] = (where[longest] + shift) % drawn.shape[longest]
        spots.append(tuple(where))
    return drawn.at[spots[0]].set(least).at[spots[1]].set(largest)


def setup_inputs(seed: int = 0) -> dict:
    splits = jax.random.split(jax.random.key(seed), 4)
    return {
        "spectra": draw_spectra(jax.random.fold_in(splits[3], 71), 0),
        "bad_channels": with_ends((jax.random.randint(splits[1], (CHANNELS,), 0, 8) < 1).astype(jnp.int32), jax.random.fold_in(splits[1], 1), 0, 1),
        "tile_list": draw_tile_list(jax.random.fold_in(splits[3], 71), 0),
    }


EPSILON = 1e-06

def whiten(spectra, bad_channels):
    values = spectra.astype(jnp.float32)
    power = lax.optimization_barrier(jnp.mean(values * values, axis=(0, 2)))
    keep_mask = (1 - bad_channels).astype(jnp.float32)
    white = values * lax.rsqrt(power + EPSILON)[None, :, None, :] * keep_mask[None, None, None, :]
    return white.astype(jnp.bfloat16)

def lag_table(hour_count):
    bin_number = jnp.arange(F, dtype=jnp.float32) + 1.0
    lag_steps = jnp.arange(LAGS, dtype=jnp.float32) - float(LAGS // 2)
    phases = math.pi / F * bin_number[:, None] * lag_steps[None, :]
    norm_scale = 1.0 / math.sqrt(F * hour_count)
    return jnp.stack([jnp.cos(phases) * norm_scale, -jnp.sin(phases) * norm_scale], axis=1)

def take_block(spectra_all, block_index):
    return lax.dynamic_slice_in_dim(spectra_all, (block_index * TILE).astype(jnp.int32), TILE, axis=3)

def cross_spec(spectra_all, tile_pair):
    left_block = take_block(spectra_all, tile_pair[0]).astype(jnp.float32)
    right_block = take_block(spectra_all, tile_pair[1]).astype(jnp.float32)
    bin_total = left_block.shape[0]
    hour_count = left_block.shape[1]
    row_block = left_block.reshape(bin_total, 2 * hour_count, TILE)
    turned = jnp.stack([-right_block[:, :, 1], right_block[:, :, 0]], axis=2)
    col_block = jnp.concatenate([right_block, turned], axis=3).reshape(bin_total, 2 * hour_count, 2 * TILE)
    return jnp.einsum('fki,fkj->fij', row_block, col_block, precision=lax.Precision.HIGHEST)

def transform(cross, table):
    parted = cross.reshape(cross.shape[0], TILE, 2, TILE)
    return jnp.einsum('fixj,fxt->tij', parted, table, precision=lax.Precision.HIGHEST)

def reference(spectra, bad_channels, tile_list):
    white = whiten(spectra, bad_channels)
    table = lag_table(HOURS)

    def tile_lags(tile_pair):
        return transform(cross_spec(white, tile_pair), table)
    return lax.map(tile_lags, tile_list)
```

```python
import functools
import math

import jax
import jax.numpy as jnp
import numpy as np
from jax import lax
from jax.experimental import pallas as pl
from jax.experimental.pallas import tpu as pltpu
from jax.sharding import PartitionSpec as P

F = 64
HOURS = 8
LAGS = 32
TILE = 128
CHANNELS = 6144
EPSILON = 1e-06

PLANE = 32
SHARD = 96
HALF_BLOCKS = 24
ROWS = 8
SLOTS = 4
MESH_ID = pl.DeviceIdType.MESH
CHUNK_OF_STEP = ((2, 0), (6, 0), (7, 1), (3, 1), (1, 2), (5, 2), (4, 3))


def exchange_kernel(
    spec_ref, bad_ref, tile_ref, out_ref,
    white, mine, tiles_in, tiles, zb0, zb1, zb2, zb3, pack,
    sem_a_send, sem_a_recv, sem_t_send, sem_t_recv, sem_t_local, sem_z_send, sem_z_recv, sem_p_send, sem_p_recv,
):
    zbs = (zb0, zb1, zb2, zb3)
    chan, tm = lax.axis_index("chan"), lax.axis_index("tm")
    half = chan // PLANE
    me = chan % PLANE
    x, y, core = me // 8, (me // 2) % 4, me % 2
    z = half * 4 + tm

    def plane_peer(j):
        dx, dy, dc = j // 8, (j // 2) % 4, j % 2
        k = ((x + dx) % 4) * 8 + ((y + dy) % 4) * 2 + (core + dc) % 2
        return k, (half * PLANE + k, tm)

    def z_peer(step):
        zz = (z + step) % 8
        return ((zz // 4) * PLANE + me, zz % 4)

    barrier = pltpu.get_barrier_semaphore()

    def greet(j, carry):
        _, dev = plane_peer(j)
        pl.semaphore_signal(barrier, inc=1, device_id=dev, device_id_type=MESH_ID)
        return carry

    lax.fori_loop(1, PLANE, greet, 0)
    for step, _ in CHUNK_OF_STEP:
        pl.semaphore_signal(barrier, inc=1, device_id=z_peer(step), device_id_type=MESH_ID)

    values = spec_ref[...].astype(jnp.float32)
    squares = jnp.sum((values * values).reshape(F // 2, ROWS, SHARD), axis=0)
    row = lax.broadcasted_iota(jnp.int32, (ROWS, SHARD), 0)
    first = (row % 4) < 2
    power0 = jnp.sum(jnp.where(first, squares, 0.0), axis=0, keepdims=True) / (2 * F)
    power1 = jnp.sum(jnp.where(first, 0.0, squares), axis=0, keepdims=True) / (2 * F)
    scale = lax.rsqrt(jnp.where(first, power0, power1) + EPSILON)
    keep = (1 - bad_ref[...]).astype(jnp.float32)
    whitened = values.reshape(F // 2, ROWS, SHARD) * scale[None] * keep[None]
    padded = jnp.concatenate([whitened, jnp.zeros((F // 2, ROWS, TILE - SHARD), jnp.float32)], axis=2)
    white[...] = padded.astype(jnp.bfloat16)

    pl.semaphore_wait(barrier, PLANE - 1 + 7)

    own_tiles = pltpu.make_async_copy(tile_ref, tiles_in.at[me], sem_t_recv)
    own_tiles.start()
    own_slice = pltpu.make_async_copy(white.at[me], mine.at[me], sem_a_recv)
    own_slice.start()

    def spread(j, carry):
        k, dev = plane_peer(j)
        pltpu.make_async_remote_copy(
            src_ref=white.at[k], dst_ref=mine.at[me], send_sem=sem_a_send, recv_sem=sem_a_recv,
            device_id=dev, device_id_type=MESH_ID,
        ).start()
        return carry

    lax.fori_loop(1, PLANE, spread, 0)

    def spread_tiles(j, carry):
        _, dev = plane_peer(j)
        pltpu.make_async_remote_copy(
            src_ref=tile_ref, dst_ref=tiles_in.at[me], send_sem=sem_t_send, recv_sem=sem_t_recv,
            device_id=dev, device_id_type=MESH_ID,
        ).start()
        return carry

    lax.fori_loop(1, PLANE, spread_tiles, 0)

    pltpu.make_async_copy(mine, mine, sem_a_recv).wait()

    lane = lax.broadcasted_iota(jnp.int32, (ROWS, TILE), 1)
    base = half * HALF_BLOCKS
    for g in range(PLANE // 4):
        s0, s1, s2, s3 = (mine[4 * g + i].astype(jnp.float32) for i in range(4))
        s1 = pltpu.roll(s1, 96, 1)
        s2 = pltpu.roll(s2, 64, 1)
        s3 = pltpu.roll(s3, 32, 1)
        zb3[base + 3 * g] = jnp.where(lane < 96, s0, s1).astype(jnp.bfloat16)
        zb3[base + 3 * g + 1] = jnp.where(lane < 64, s1, s2).astype(jnp.bfloat16)
        zb3[base + 3 * g + 2] = jnp.where(lane < 32, s2, s3).astype(jnp.bfloat16)

    for step, chunk in CHUNK_OF_STEP:
        pltpu.make_async_remote_copy(
            src_ref=zb3.at[pl.ds(base, HALF_BLOCKS)], dst_ref=zbs[chunk].at[pl.ds(base, HALF_BLOCKS)],
            send_sem=sem_z_send, recv_sem=sem_z_recv.at[chunk],
            device_id=z_peer(step), device_id_type=MESH_ID,
        ).start()

    pltpu.make_async_copy(tiles_in, tiles_in, sem_t_recv).wait()
    to_smem = pltpu.make_async_copy(tiles_in, tiles, sem_t_local)
    to_smem.start()
    to_smem.wait()

    for chunk in range(4):
        t = (tm + (2, 1, 3, 0)[chunk]) % 4
        zb = zbs[chunk]
        if chunk < 3:
            pltpu.make_async_copy(zb, zb, sem_z_recv.at[chunk]).wait()
        else:
            other = zb.at[pl.ds((1 - half) * HALF_BLOCKS, HALF_BLOCKS)]
            pltpu.make_async_copy(other, other, sem_z_recv.at[chunk]).wait()

        def select(j, carry):
            k, _ = plane_peer(j)
            for s in range(SLOTS):
                pack[chunk, k, s] = zb[tiles[k, 0, SLOTS * tm + s]]
            return carry

        lax.fori_loop(0, PLANE, select, 0)
        pltpu.make_async_copy(pack.at[chunk, me], out_ref.at[t, me], sem_p_recv).start()

        def deliver(j, carry):
            k, dev = plane_peer(j)
            pltpu.make_async_remote_copy(
                src_ref=pack.at[chunk, k], dst_ref=out_ref.at[t, me], send_sem=sem_p_send, recv_sem=sem_p_recv,
                device_id=dev, device_id_type=MESH_ID,
            ).start()
            return carry

        lax.fori_loop(1, PLANE, deliver, 0)

    pltpu.make_async_copy(out_ref, out_ref, sem_p_recv).wait()
    sent = white.at[pl.ds(0, PLANE - 1)]
    pltpu.make_async_copy(sent, sent, sem_a_send).wait()
    sent = tiles_in.at[pl.ds(0, PLANE - 1)]
    pltpu.make_async_copy(sent, sent, sem_t_send).wait()
    for _ in CHUNK_OF_STEP:
        sent = zb3.at[pl.ds(0, HALF_BLOCKS)]
        pltpu.make_async_copy(sent, sent, sem_z_send).wait()
    sent = pack.at[:, pl.ds(0, PLANE - 1)]
    pltpu.make_async_copy(sent, sent, sem_p_send).wait()


def exchange(spectra, bad, tile_row):
    vmem = pl.BlockSpec(memory_space=pltpu.VMEM)
    slab = pltpu.VMEM((2 * HALF_BLOCKS, ROWS, TILE), jnp.bfloat16)
    return pl.pallas_call(
        exchange_kernel,
        out_shape=jax.ShapeDtypeStruct((4, PLANE, SLOTS, ROWS, TILE), jnp.bfloat16),
        in_specs=[vmem, vmem, vmem],
        out_specs=pl.BlockSpec(memory_space=pl.ANY),
        scratch_shapes=[
            pltpu.VMEM((PLANE, ROWS, TILE), jnp.bfloat16),
            pltpu.VMEM((PLANE, ROWS, TILE), jnp.bfloat16),
            pltpu.VMEM((PLANE, 1, TILE), jnp.int32),
            pltpu.SMEM((PLANE, 1, TILE), jnp.int32),
            slab, slab, slab, slab,
            pltpu.VMEM((4, PLANE, SLOTS, ROWS, TILE), jnp.bfloat16),
            pltpu.SemaphoreType.DMA, pltpu.SemaphoreType.DMA,
            pltpu.SemaphoreType.DMA, pltpu.SemaphoreType.DMA, pltpu.SemaphoreType.DMA,
            pltpu.SemaphoreType.DMA, pltpu.SemaphoreType.DMA((4,)),
            pltpu.SemaphoreType.DMA, pltpu.SemaphoreType.DMA,
        ],
        compiler_params=pltpu.CompilerParams(collective_id=0, has_side_effects=True),
        name="exchange",
    )(spectra, bad, tile_row)


def lag_tables():
    row = np.arange(F * HOURS * 2)
    bin_number = 2 * ((row // ROWS) % PLANE) + (row % ROWS) // 4 + 1.0
    phase = np.pi / F * bin_number[None, :] * np.arange(17)[:, None]
    norm = 1.0 / math.sqrt(F * HOURS)
    return np.stack([np.cos(phase) * norm, np.sin(phase) * norm], axis=1).astype(np.float32)


def correlate_kernel(blocks_ref, table_ref, out_ref, left, right, turned):
    rows = F * HOURS * 2
    a = blocks_ref[:, :, 0].astype(jnp.float32).reshape(rows, TILE)
    left[...] = a.T
    b = blocks_ref[:, :, 1].astype(jnp.float32).reshape(rows, TILE)
    right[...] = b.astype(jnp.bfloat16)
    part = lax.broadcasted_iota(jnp.int32, (rows, TILE), 0) % 2
    turned[...] = jnp.where(part == 0, -pltpu.roll(b, rows - 1, 0), pltpu.roll(b, 1, 0)).astype(jnp.bfloat16)
    for m in range(17):
        cosines = (left[...] * table_ref[m, 0:1]).astype(jnp.bfloat16)
        c = jnp.dot(cosines, right[...], preferred_element_type=jnp.float32)
        if m == 0:
            out_ref[0, LAGS // 2] = c
            continue
        sines = (left[...] * table_ref[m, 1:2]).astype(jnp.bfloat16)
        d = jnp.dot(sines, turned[...], preferred_element_type=jnp.float32)
        if m < LAGS // 2:
            out_ref[0, LAGS // 2 + m] = c - d
        out_ref[0, LAGS // 2 - m] = c + d


def correlate(blocks, table):
    rows = F * HOURS * 2
    return pl.pallas_call(
        correlate_kernel,
        grid=(2,),
        out_shape=jax.ShapeDtypeStruct((2, LAGS, TILE, TILE), jnp.float32),
        in_specs=[
            pl.BlockSpec((4, PLANE, 2, ROWS, TILE), lambda i: (0, 0, i, 0, 0)),
            pl.BlockSpec((17, 2, rows), lambda i: (0, 0, 0)),
        ],
        out_specs=pl.BlockSpec((1, LAGS, TILE, TILE), lambda i: (i, 0, 0, 0)),
        scratch_shapes=[
            pltpu.VMEM((TILE, rows), jnp.float32),
            pltpu.VMEM((rows, TILE), jnp.bfloat16),
            pltpu.VMEM((rows, TILE), jnp.bfloat16),
        ],
        name="correlate",
    )(blocks, table)


def per_device(spectra, bad_channels, tile_list):
    rows = spectra.reshape(F * 2 * 2, SHARD)
    tile_row = jnp.pad(tile_list.reshape(1, 16), ((0, 0), (0, TILE - 16)))
    blocks = exchange(rows, bad_channels.reshape(1, SHARD), tile_row)
    return correlate(blocks, jnp.asarray(lag_tables()))


def solution(mesh):
    placed = (P(None, "tm", None, "chan"), P("chan"), P("chan", None))
    return jax.shard_map(
        per_device,
        mesh=mesh,
        in_specs=placed,
        out_specs=P(("chan", "tm"), None, None, None),
        check_vma=False,
    )
```

```python
import math

import jax
import jax.numpy as jnp
import numpy as np
from jax import lax
from jax.experimental import pallas as pl
from jax.experimental.pallas import tpu as pltpu
from jax.sharding import PartitionSpec as P

F = 64
HOURS = 8
LAGS = 32
TILE = 128
EPSILON = 1e-06

PLANE = 32
SHARD = 96
HALF = 24
ROWS = 8
DEPTH = PLANE * ROWS
SLOTS = 4
FINE = 4
COARSE = LAGS // FINE
MESH_ID = pl.DeviceIdType.MESH


def fused_kernel(
    spec_hbm, bad_ref, tile_ref, left_table, right_table, out_ref,
    spec, white, mine, tiles_in, tiles, zb0, zb1, zb2, zb3, pack, got, cosines, sines, lhs, rhs,
    sem_in, sem_a_send, sem_a_recv, sem_t_send, sem_t_recv, sem_t_local, sem_z_send, sem_z_recv,
    sem_p_send, sem_p_recv,
):
    zbs = (zb0, zb1, zb2, zb3)
    chan, tm = lax.axis_index("chan"), lax.axis_index("tm")
    half = chan // PLANE
    me = chan % PLANE
    x, y, core = me // 8, (me // 2) % 4, me % 2
    z = half * 4 + tm

    load = pltpu.make_async_copy(spec_hbm, spec, sem_in)
    load.start()

    def plane_peer(j):
        dx, dy, dc = j // 8, (j // 2) % 4, j % 2
        k = ((x + dx) % 4) * 8 + ((y + dy) % 4) * 2 + (core + dc) % 2
        return k, (half * PLANE + k, tm)

    def plane(step):
        return (z + step) % 8

    def z_peer(step):
        return (plane(step) // 4) * PLANE + me, plane(step) % 4

    def base(step):
        return (plane(step) // 4) * HALF

    barrier = pltpu.get_barrier_semaphore()

    def greet(j, carry):
        _, dev = plane_peer(j)
        pl.semaphore_signal(barrier, inc=1, device_id=dev, device_id_type=MESH_ID)
        return carry

    lax.fori_loop(1, PLANE, greet, 0)
    for step in (2, 6, 1, 7):
        pl.semaphore_signal(barrier, inc=1, device_id=z_peer(step), device_id_type=MESH_ID)

    load.wait()
    values = spec[...].astype(jnp.float32).reshape(F // 2, ROWS, SHARD)
    squares = jnp.sum(values * values, axis=0)
    row = lax.broadcasted_iota(jnp.int32, (ROWS, SHARD), 0)
    first = (row % 4) < 2
    power0 = jnp.sum(jnp.where(first, squares, 0.0), axis=0, keepdims=True) / (2 * F)
    power1 = jnp.sum(jnp.where(first, 0.0, squares), axis=0, keepdims=True) / (2 * F)
    scale = lax.rsqrt(jnp.where(first, power0, power1) + EPSILON)
    keep = (1 - bad_ref[...]).astype(jnp.float32)
    whitened = values * scale[None] * keep[None]
    padded = jnp.concatenate([whitened, jnp.zeros((F // 2, ROWS, TILE - SHARD), jnp.float32)], axis=2)
    white[...] = padded.astype(jnp.bfloat16)

    pl.semaphore_wait(barrier, PLANE - 1 + 4)

    pltpu.make_async_copy(white.at[me], mine.at[me], sem_a_recv).start()

    def spread(j, carry):
        k, dev = plane_peer(j)
        pltpu.make_async_remote_copy(
            src_ref=white.at[k], dst_ref=mine.at[me], send_sem=sem_a_send, recv_sem=sem_a_recv,
            device_id=dev, device_id_type=MESH_ID,
        ).start()
        return carry

    lax.fori_loop(1, PLANE, spread, 0)

    pltpu.make_async_copy(tile_ref, tiles_in.at[me], sem_t_recv).start()

    def spread_tiles(j, carry):
        _, dev = plane_peer(j)
        pltpu.make_async_remote_copy(
            src_ref=tile_ref, dst_ref=tiles_in.at[me], send_sem=sem_t_send, recv_sem=sem_t_recv,
            device_id=dev, device_id_type=MESH_ID,
        ).start()
        return carry

    lax.fori_loop(1, PLANE, spread_tiles, 0)

    out_ref[...] = jnp.zeros_like(out_ref)
    for fine in range(1, FINE):
        column = 2 * (fine - 1)
        cosines[fine - 1] = jnp.broadcast_to(right_table[:, column : column + 1], (DEPTH, TILE))
        sines[fine - 1] = jnp.broadcast_to(right_table[:, column + 1 : column + 2], (DEPTH, TILE))

    pltpu.make_async_copy(mine, mine, sem_a_recv).wait()

    lane = lax.broadcasted_iota(jnp.int32, (ROWS, TILE), 1)
    own = half * HALF
    for g in range(PLANE // 4):
        s0, s1, s2, s3 = (mine[4 * g + i].astype(jnp.float32) for i in range(4))
        s1 = pltpu.roll(s1, 96, 1)
        s2 = pltpu.roll(s2, 64, 1)
        s3 = pltpu.roll(s3, 32, 1)
        zb3[own + 3 * g] = jnp.where(lane < 96, s0, s1).astype(jnp.bfloat16)
        zb3[own + 3 * g + 1] = jnp.where(lane < 64, s1, s2).astype(jnp.bfloat16)
        zb3[own + 3 * g + 2] = jnp.where(lane < 32, s2, s3).astype(jnp.bfloat16)

    def send_z(src, dst, chunk, at, count, step):
        pltpu.make_async_remote_copy(
            src_ref=src.at[pl.ds(at, count)], dst_ref=dst.at[pl.ds(at, count)],
            send_sem=sem_z_send, recv_sem=sem_z_recv.at[chunk],
            device_id=z_peer(step), device_id_type=MESH_ID,
        ).start()

    for step, chunk in ((2, 0), (6, 0), (7, 1), (1, 2)):
        send_z(zb3, zbs[chunk], chunk, own, HALF, step)

    pltpu.make_async_copy(tiles_in, tiles_in, sem_t_recv).wait()
    to_smem = pltpu.make_async_copy(tiles_in, tiles, sem_t_local)
    to_smem.start()
    to_smem.wait()

    for chunk in range(4):
        zb = zbs[chunk]
        if chunk < 3:
            pltpu.make_async_copy(zb, zb, sem_z_recv.at[chunk]).wait()
        else:
            other = zb.at[pl.ds((1 - half) * HALF, HALF)]
            pltpu.make_async_copy(other, other, sem_z_recv.at[chunk]).wait()
        if chunk == 0:
            send_z(zb0, zb1, 1, base(6), HALF, 1)
            send_z(zb0, zb2, 2, base(2), HALF, 7)
            send_z(zb0, zb3, 3, base(6), HALF // 2, 2)
            send_z(zb0, zb3, 3, base(2) + HALF // 2, HALF // 2, 6)

        def select(j, carry):
            k, _ = plane_peer(j)
            for s in range(SLOTS):
                pack[chunk, k, s] = zb[tiles[k, s % 2, 2 * tm + s // 2]]
            return carry

        lax.fori_loop(0, PLANE, select, 0)
        pltpu.make_async_copy(pack.at[chunk, me], got.at[chunk, me], sem_p_recv.at[chunk]).start()

        def deliver(j, carry):
            k, dev = plane_peer(j)
            pltpu.make_async_remote_copy(
                src_ref=pack.at[chunk, k], dst_ref=got.at[chunk, me],
                send_sem=sem_p_send, recv_sem=sem_p_recv.at[chunk],
                device_id=dev, device_id_type=MESH_ID,
            ).start()
            return carry

        lax.fori_loop(1, PLANE, deliver, 0)

    even_lane = lax.broadcasted_iota(jnp.int32, (TILE, TILE), 1) % 2 == 0
    even_row = lax.broadcasted_iota(jnp.int32, (PLANE, ROWS, TILE), 1) % 2 == 0

    def correlate(chunk, carry):
        part = got.at[chunk]
        pltpu.make_async_copy(part, part, sem_p_recv.at[chunk]).wait()

        def one_tile(i, carry):
            a = got[chunk, :, 2 * i].astype(jnp.float32).reshape(DEPTH, TILE)
            for h in range(DEPTH // TILE):
                block = a[h * TILE : (h + 1) * TILE].T
                turned = jnp.where(even_lane, -pltpu.roll(block, TILE - 1, 1), pltpu.roll(block, 1, 1))
                cols = pl.ds(h * TILE, TILE)
                for c in range(COARSE):
                    cos = left_table[2 * c : 2 * c + 1, h * TILE : (h + 1) * TILE]
                    sin = left_table[2 * c + 1 : 2 * c + 2, h * TILE : (h + 1) * TILE]
                    lhs[pl.ds(c * TILE, TILE), cols] = (block * cos + turned * sin).astype(jnp.bfloat16)
            b = got[chunk, :, 2 * i + 1].astype(jnp.float32)
            turned = jnp.where(even_row, pltpu.roll(b, ROWS - 1, 1), -pltpu.roll(b, 1, 1)).reshape(DEPTH, TILE)
            b = b.reshape(DEPTH, TILE)
            rhs[:, 0:TILE] = b.astype(jnp.bfloat16)
            for fine in range(1, FINE):
                rotated = b * cosines[fine - 1] + turned * sines[fine - 1]
                rhs[:, fine * TILE : (fine + 1) * TILE] = rotated.astype(jnp.bfloat16)
            for n in range(2):
                weights = rhs[:, 2 * n * TILE : (2 * n + 2) * TILE]
                for c in range(0, COARSE, 2):
                    res = jnp.dot(lhs[c * TILE : (c + 2) * TILE, :], weights, preferred_element_type=jnp.float32)
                    for dc in range(2):
                        for dn in range(2):
                            lag = FINE * (c + dc) + 2 * n + dn
                            out_ref[i, lag] += res[dc * TILE : (dc + 1) * TILE, dn * TILE : (dn + 1) * TILE]
            return carry

        return lax.fori_loop(0, 2, one_tile, carry)

    lax.fori_loop(0, 4, correlate, 0)

    sent = white.at[pl.ds(0, PLANE - 1)]
    pltpu.make_async_copy(sent, sent, sem_a_send).wait()
    sent = tiles_in.at[pl.ds(0, PLANE - 1)]
    pltpu.make_async_copy(sent, sent, sem_t_send).wait()
    for _ in range(7):
        sent = zb3.at[pl.ds(0, HALF)]
        pltpu.make_async_copy(sent, sent, sem_z_send).wait()
    sent = pack.at[:, pl.ds(0, PLANE - 1)]
    pltpu.make_async_copy(sent, sent, sem_p_send).wait()


def fused(spectra, bad, tile_pairs):
    vmem = pl.BlockSpec(memory_space=pltpu.VMEM)
    slab = pltpu.VMEM((2 * HALF, ROWS, TILE), jnp.bfloat16)
    dma = pltpu.SemaphoreType.DMA
    left_table, right_table = lag_tables()
    return pl.pallas_call(
        fused_kernel,
        out_shape=jax.ShapeDtypeStruct((2, LAGS, TILE, TILE), jnp.float32),
        in_specs=[pl.BlockSpec(memory_space=pl.ANY), vmem, vmem, vmem, vmem],
        out_specs=vmem,
        scratch_shapes=[
            pltpu.VMEM((F * 4, SHARD), jnp.bfloat16),
            pltpu.VMEM((PLANE, ROWS, TILE), jnp.bfloat16),
            pltpu.VMEM((PLANE, ROWS, TILE), jnp.bfloat16),
            pltpu.VMEM((PLANE, 2, 8), jnp.int32),
            pltpu.SMEM((PLANE, 2, 8), jnp.int32),
            slab, slab, slab, slab,
            pltpu.VMEM((4, PLANE, SLOTS, ROWS, TILE), jnp.bfloat16),
            pltpu.VMEM((4, PLANE, SLOTS, ROWS, TILE), jnp.bfloat16),
            pltpu.VMEM((FINE - 1, DEPTH, TILE), jnp.float32),
            pltpu.VMEM((FINE - 1, DEPTH, TILE), jnp.float32),
            pltpu.VMEM((COARSE * TILE, DEPTH), jnp.bfloat16),
            pltpu.VMEM((DEPTH, FINE * TILE), jnp.bfloat16),
            dma, dma, dma, dma, dma, dma, dma, dma((4,)), dma, dma((4,)),
        ],
        compiler_params=pltpu.CompilerParams(
            collective_id=0, has_side_effects=True, vmem_limit_bytes=16 << 20
        ),
        name="fused",
    )(spectra, bad, tile_pairs, jnp.asarray(left_table), jnp.asarray(right_table))


def lag_tables():
    row = np.arange(DEPTH)
    bin_number = 2 * (row // ROWS) + (row % ROWS) // 4 + 1.0
    angle = np.pi / F * bin_number
    coarse = FINE * np.arange(COARSE) - LAGS // 2
    norm = 1.0 / math.sqrt(F * HOURS)
    left = np.stack([np.cos(coarse[:, None] * angle), np.sin(coarse[:, None] * angle)], axis=1) * norm
    right = np.zeros((DEPTH, TILE))
    for fine in range(1, FINE):
        right[:, 2 * fine - 2] = np.cos(fine * angle)
        right[:, 2 * fine - 1] = np.sin(fine * angle)
    return left.reshape(2 * COARSE, DEPTH).astype(np.float32), right.astype(np.float32)


def per_device(spectra, bad_channels, tile_list):
    rows = spectra.reshape(F * 4, SHARD)
    return fused(rows, bad_channels.reshape(1, SHARD), tile_list.T)


def solution(mesh):
    placed = (P(None, "tm", None, "chan"), P("chan"), P("chan", None))
    return jax.shard_map(
        per_device,
        mesh=mesh,
        in_specs=placed,
        out_specs=P(("chan", "tm"), None, None, None),
        check_vma=False,
    )
```

```python
import math

import jax
import jax.numpy as jnp
import numpy as np
from jax import lax
from jax.experimental import pallas as pl
from jax.experimental.pallas import tpu as pltpu
from jax.sharding import PartitionSpec as P

F = 64
HOURS = 8
LAGS = 32
TILE = 128
EPSILON = 1e-06

PLANE = 32
SHARD = 96
HALF = 24
ROWS = 8
DEPTH = PLANE * ROWS
SLOTS = 4
FINE = 4
COARSE = LAGS // FINE
FAR = 20
MESH_ID = pl.DeviceIdType.MESH


def fused_kernel(
    spec_hbm, bad_hbm, tile_hbm, left_hbm, right_hbm, out_ref,
    spec, bad_ref, tile_ref, left_table, right_table, white, mine, tiles_in, tiles, zb0, zb1, zb2, zb3, pack, got, cosines, sines, lhs, rhs,
    sem_in, sem_a_send, sem_a_recv, sem_t_send, sem_t_recv, sem_t_local, sem_z_send, sem_z_recv,
    sem_p_send, sem_p_recv,
):
    zbs = (zb0, zb1, zb2, zb3)
    chan, tm = lax.axis_index("chan"), lax.axis_index("tm")
    half = lax.shift_right_logical(chan, 5)
    me = lax.bitwise_and(chan, PLANE - 1)
    z = half * 4 + tm

    loads = [
        pltpu.make_async_copy(src, dst, sem_in.at[i])
        for i, (src, dst) in enumerate(
            ((spec_hbm, spec), (bad_hbm, bad_ref), (tile_hbm, tile_ref), (left_hbm, left_table), (right_hbm, right_table))
        )
    ]
    for load in loads:
        load.start()

    def plane_peer(j):
        k = lax.bitwise_xor(me, j)
        return k, (lax.bitwise_xor(chan, j), tm)

    def each_peer(act):
        def four(i, carry):
            for u in range(4):
                act(lax.bitwise_xor(4 * i + u, FAR))
            return carry

        lax.fori_loop(0, FAR // 4, four, 0)
        for u in range(FAR + 1, FAR + 4):
            act(u ^ FAR)
        lax.fori_loop(FAR // 4 + 1, PLANE // 4, four, 0)

    def plane(step):
        return lax.bitwise_and(z + step, 7)

    def z_peer(step):
        zz = plane(step)
        return lax.shift_right_logical(zz, 2) * PLANE + me, lax.bitwise_and(zz, 3)

    def base(step):
        return lax.shift_right_logical(plane(step), 2) * HALF

    barrier = pltpu.get_barrier_semaphore()

    def greet(j):
        _, dev = plane_peer(j)
        pl.semaphore_signal(barrier, inc=1, device_id=dev, device_id_type=MESH_ID)

    each_peer(greet)
    for step in (2, 6, 1, 7):
        pl.semaphore_signal(barrier, inc=1, device_id=z_peer(step), device_id_type=MESH_ID)

    for load in loads[:2]:
        load.wait()
    values = spec[...].astype(jnp.float32).reshape(F // 2, ROWS, SHARD)
    squares = jnp.sum(values * values, axis=0)
    row = lax.broadcasted_iota(jnp.int32, (ROWS, SHARD), 0)
    first = (row % 4) < 2
    power0 = jnp.sum(jnp.where(first, squares, 0.0), axis=0, keepdims=True) / (2 * F)
    power1 = jnp.sum(jnp.where(first, 0.0, squares), axis=0, keepdims=True) / (2 * F)
    scale = lax.rsqrt(jnp.where(first, power0, power1) + EPSILON)
    keep = (1 - bad_ref[...]).astype(jnp.float32)
    whitened = values * scale[None] * keep[None]
    padded = jnp.concatenate([whitened, jnp.zeros((F // 2, ROWS, TILE - SHARD), jnp.float32)], axis=2)
    white[...] = padded.astype(jnp.bfloat16)

    pl.semaphore_wait(barrier, PLANE - 1 + 4)

    pltpu.make_async_copy(white.at[me], mine.at[me], sem_a_recv).start()

    def spread(j):
        k, dev = plane_peer(j)
        pltpu.make_async_remote_copy(
            src_ref=white.at[k], dst_ref=mine.at[me], send_sem=sem_a_send, recv_sem=sem_a_recv,
            device_id=dev, device_id_type=MESH_ID,
        ).start()

    each_peer(spread)

    for load in loads[2:]:
        load.wait()
    pltpu.make_async_copy(tile_ref, tiles_in.at[me], sem_t_recv).start()

    def spread_tiles(j):
        _, dev = plane_peer(j)
        pltpu.make_async_remote_copy(
            src_ref=tile_ref, dst_ref=tiles_in.at[me], send_sem=sem_t_send, recv_sem=sem_t_recv,
            device_id=dev, device_id_type=MESH_ID,
        ).start()

    each_peer(spread_tiles)

    out_ref[...] = jnp.zeros_like(out_ref)
    for fine in range(1, FINE):
        column = 2 * (fine - 1)
        cosines[fine - 1] = jnp.broadcast_to(right_table[:, column : column + 1], (DEPTH, TILE))
        sines[fine - 1] = jnp.broadcast_to(right_table[:, column + 1 : column + 2], (DEPTH, TILE))

    pltpu.make_async_copy(mine, mine, sem_a_recv).wait()

    lane = lax.broadcasted_iota(jnp.int32, (ROWS, TILE), 1)
    own = half * HALF
    for g in range(PLANE // 4):
        s0, s1, s2, s3 = (mine[4 * g + i].astype(jnp.float32) for i in range(4))
        s1 = pltpu.roll(s1, 96, 1)
        s2 = pltpu.roll(s2, 64, 1)
        s3 = pltpu.roll(s3, 32, 1)
        zb3[own + 3 * g] = jnp.where(lane < 96, s0, s1).astype(jnp.bfloat16)
        zb3[own + 3 * g + 1] = jnp.where(lane < 64, s1, s2).astype(jnp.bfloat16)
        zb3[own + 3 * g + 2] = jnp.where(lane < 32, s2, s3).astype(jnp.bfloat16)

    def send_z(src, dst, chunk, at, count, step):
        pltpu.make_async_remote_copy(
            src_ref=src.at[pl.ds(at, count)], dst_ref=dst.at[pl.ds(at, count)],
            send_sem=sem_z_send, recv_sem=sem_z_recv.at[chunk],
            device_id=z_peer(step), device_id_type=MESH_ID,
        ).start()

    for step, chunk in ((2, 0), (6, 0), (7, 1), (1, 2)):
        send_z(zb3, zbs[chunk], chunk, own, HALF, step)

    pltpu.make_async_copy(tiles_in, tiles_in, sem_t_recv).wait()
    to_smem = pltpu.make_async_copy(tiles_in, tiles, sem_t_local)
    to_smem.start()
    to_smem.wait()

    for chunk in range(4):
        zb = zbs[chunk]
        if chunk < 3:
            pltpu.make_async_copy(zb, zb, sem_z_recv.at[chunk]).wait()
        else:
            other = zb.at[pl.ds((1 - half) * HALF, HALF)]
            pltpu.make_async_copy(other, other, sem_z_recv.at[chunk]).wait()
        if chunk == 0:
            send_z(zb0, zb1, 1, base(6), HALF, 1)
            send_z(zb0, zb2, 2, base(2), HALF, 7)
            send_z(zb0, zb3, 3, base(6), HALF // 2, 2)
            send_z(zb0, zb3, 3, base(2) + HALF // 2, HALF // 2, 6)

        def select(i, carry):
            places = [(4 * i + u, s) for u in range(4) for s in range(SLOTS)]
            blocks = [zb[tiles[k, s % 2, 2 * tm + s // 2]] for k, s in places]
            for (k, s), block in zip(places, blocks):
                pack[chunk, k, s] = block
            return carry

        lax.fori_loop(0, PLANE // 4, select, 0)
        pltpu.make_async_copy(pack.at[chunk, me], got.at[chunk, me], sem_p_recv.at[chunk]).start()

        def deliver(j):
            k, dev = plane_peer(j)
            pltpu.make_async_remote_copy(
                src_ref=pack.at[chunk, k], dst_ref=got.at[chunk, me],
                send_sem=sem_p_send, recv_sem=sem_p_recv.at[chunk],
                device_id=dev, device_id_type=MESH_ID,
            ).start()

        each_peer(deliver)

    even_lane = lax.broadcasted_iota(jnp.int32, (TILE, TILE), 1) % 2 == 0
    even_row = lax.broadcasted_iota(jnp.int32, (PLANE, ROWS, TILE), 1) % 2 == 0

    def correlate(chunk, carry):
        part = got.at[chunk]
        pltpu.make_async_copy(part, part, sem_p_recv.at[chunk]).wait()

        def one_tile(i, carry):
            a = got[chunk, :, 2 * i].astype(jnp.float32).reshape(DEPTH, TILE)
            for h in range(DEPTH // TILE):
                block = a[h * TILE : (h + 1) * TILE].T
                turned = jnp.where(even_lane, -pltpu.roll(block, TILE - 1, 1), pltpu.roll(block, 1, 1))
                cols = pl.ds(h * TILE, TILE)
                for c in range(COARSE):
                    cos = left_table[2 * c : 2 * c + 1, h * TILE : (h + 1) * TILE]
                    sin = left_table[2 * c + 1 : 2 * c + 2, h * TILE : (h + 1) * TILE]
                    lhs[pl.ds(c * TILE, TILE), cols] = (block * cos + turned * sin).astype(jnp.bfloat16)
            b = got[chunk, :, 2 * i + 1].astype(jnp.float32)
            turned = jnp.where(even_row, pltpu.roll(b, ROWS - 1, 1), -pltpu.roll(b, 1, 1)).reshape(DEPTH, TILE)
            b = b.reshape(DEPTH, TILE)
            rhs[:, 0:TILE] = b.astype(jnp.bfloat16)
            for fine in range(1, FINE):
                rotated = b * cosines[fine - 1] + turned * sines[fine - 1]
                rhs[:, fine * TILE : (fine + 1) * TILE] = rotated.astype(jnp.bfloat16)
            for n in range(2):
                weights = rhs[:, 2 * n * TILE : (2 * n + 2) * TILE]
                for c in range(0, COARSE, 2):
                    res = jnp.dot(lhs[c * TILE : (c + 2) * TILE, :], weights, preferred_element_type=jnp.float32)
                    for dc in range(2):
                        for dn in range(2):
                            lag = FINE * (c + dc) + 2 * n + dn
                            out_ref[i, lag] += res[dc * TILE : (dc + 1) * TILE, dn * TILE : (dn + 1) * TILE]
            return carry

        return lax.fori_loop(0, 2, one_tile, carry)

    lax.fori_loop(0, 4, correlate, 0)

    sent = white.at[pl.ds(0, PLANE - 1)]
    pltpu.make_async_copy(sent, sent, sem_a_send).wait()
    sent = tiles_in.at[pl.ds(0, PLANE - 1)]
    pltpu.make_async_copy(sent, sent, sem_t_send).wait()
    for _ in range(7):
        sent = zb3.at[pl.ds(0, HALF)]
        pltpu.make_async_copy(sent, sent, sem_z_send).wait()
    sent = pack.at[:, pl.ds(0, PLANE - 1)]
    pltpu.make_async_copy(sent, sent, sem_p_send).wait()


def fused(spectra, bad, tile_pairs):
    vmem = pl.BlockSpec(memory_space=pltpu.VMEM)
    slab = pltpu.VMEM((2 * HALF, ROWS, TILE), jnp.bfloat16)
    dma = pltpu.SemaphoreType.DMA
    left_table, right_table = lag_tables()
    return pl.pallas_call(
        fused_kernel,
        out_shape=jax.ShapeDtypeStruct((2, LAGS, TILE, TILE), jnp.float32),
        in_specs=[pl.BlockSpec(memory_space=pltpu.HBM)] * 5,
        out_specs=vmem,
        scratch_shapes=[
            pltpu.VMEM((F * 4, SHARD), jnp.bfloat16),
            pltpu.VMEM((1, SHARD), jnp.int32),
            pltpu.VMEM((2, 8), jnp.int32),
            pltpu.VMEM((2 * COARSE, DEPTH), jnp.float32),
            pltpu.VMEM((DEPTH, TILE), jnp.float32),
            pltpu.VMEM((PLANE, ROWS, TILE), jnp.bfloat16),
            pltpu.VMEM((PLANE, ROWS, TILE), jnp.bfloat16),
            pltpu.VMEM((PLANE, 2, 8), jnp.int32),
            pltpu.SMEM((PLANE, 2, 8), jnp.int32),
            slab, slab, slab, slab,
            pltpu.VMEM((4, PLANE, SLOTS, ROWS, TILE), jnp.bfloat16),
            pltpu.VMEM((4, PLANE, SLOTS, ROWS, TILE), jnp.bfloat16),
            pltpu.VMEM((FINE - 1, DEPTH, TILE), jnp.float32),
            pltpu.VMEM((FINE - 1, DEPTH, TILE), jnp.float32),
            pltpu.VMEM((COARSE * TILE, DEPTH), jnp.bfloat16),
            pltpu.VMEM((DEPTH, FINE * TILE), jnp.bfloat16),
            dma((5,)), dma, dma, dma, dma, dma, dma, dma((4,)), dma, dma((4,)),
        ],
        compiler_params=pltpu.CompilerParams(
            collective_id=0, has_side_effects=True, vmem_limit_bytes=16 << 20
        ),
        name="fused",
    )(*(pltpu.with_memory_space_constraint(v, pltpu.HBM) for v in (spectra, bad, tile_pairs, jnp.asarray(left_table), jnp.asarray(right_table))))


def lag_tables():
    row = np.arange(DEPTH)
    bin_number = 2 * (row // ROWS) + (row % ROWS) // 4 + 1.0
    angle = np.pi / F * bin_number
    coarse = FINE * np.arange(COARSE) - LAGS // 2
    norm = 1.0 / math.sqrt(F * HOURS)
    left = np.stack([np.cos(coarse[:, None] * angle), np.sin(coarse[:, None] * angle)], axis=1) * norm
    right = np.zeros((DEPTH, TILE))
    for fine in range(1, FINE):
        right[:, 2 * fine - 2] = np.cos(fine * angle)
        right[:, 2 * fine - 1] = np.sin(fine * angle)
    return left.reshape(2 * COARSE, DEPTH).astype(np.float32), right.astype(np.float32)


def per_device(spectra, bad_channels, tile_list):
    rows = spectra.reshape(F * 4, SHARD)
    return fused(rows, bad_channels.reshape(1, SHARD), tile_list.T)


def solution(mesh):
    placed = (P(None, "tm", None, "chan"), P("chan"), P("chan", None))
    return jax.shard_map(
        per_device,
        mesh=mesh,
        in_specs=placed,
        out_specs=P(("chan", "tm"), None, None, None),
        check_vma=False,
    )
```

```python
import math

import jax
import jax.numpy as jnp
import numpy as np
from jax import lax
from jax.experimental import pallas as pl
from jax.experimental.pallas import tpu as pltpu
from jax.sharding import PartitionSpec as P

F = 64
HOURS = 8
LAGS = 32
TILE = 128
EPSILON = 1e-06

PLANE = 32
SHARD = 96
HALF = 24
ROWS = 8
DEPTH = PLANE * ROWS
SLOTS = 4
FINE = 4
COARSE = LAGS // FINE
FAR = 20
NEAR = (0, 2, 6, 8, 24)
CROSS = tuple((near + dc, dc) for near in NEAR for dc in range(2))
INSIDE = tuple(j for j in range(PLANE) if (j & ~1) ^ FAR not in NEAR)
MESH_ID = pl.DeviceIdType.MESH


def fused_kernel(
    spec_hbm, bad_hbm, tile_hbm, left_hbm, right_hbm, out_ref,
    spec, bad_ref, tile_ref, left_table, right_table, white, mine, tiles_in, tiles, zb0, zb1, zb2, zb3, pack, got, cosines, sines, lhs, rhs, other,
    sem_in, sem_a_send, sem_a_recv, sem_t_send, sem_t_recv, sem_t_local, sem_z_send, sem_z_recv,
    sem_p_send, sem_p_recv,
):
    zbs = (zb0, zb1, zb2, zb3)
    chan, tm = lax.axis_index("chan"), lax.axis_index("tm")
    half = lax.shift_right_logical(chan, 5)
    me = lax.bitwise_and(chan, PLANE - 1)
    z = half * 4 + tm
    odd = lax.bitwise_and(z, 1)

    loads = [
        pltpu.make_async_copy(src, dst, sem_in.at[i])
        for i, (src, dst) in enumerate(
            ((spec_hbm, spec), (bad_hbm, bad_ref), (tile_hbm, tile_ref), (left_hbm, left_table), (right_hbm, right_table))
        )
    ]
    for load in loads:
        load.start()

    def plane_peer(j):
        k = lax.bitwise_xor(me, j)
        return k, (lax.bitwise_xor(chan, j), tm)

    def each_peer(act):
        def four(i, carry):
            for u in range(4):
                act(lax.bitwise_xor(4 * i + u, FAR))
            return carry

        lax.fori_loop(0, FAR // 4, four, 0)
        for u in range(FAR + 1, FAR + 4):
            act(u ^ FAR)
        lax.fori_loop(FAR // 4 + 1, PLANE // 4, four, 0)

    def plane(step):
        return lax.bitwise_and(z + step, 7)

    def z_peer(step, j=0):
        zz = plane(step)
        return lax.shift_right_logical(zz, 2) * PLANE + lax.bitwise_xor(me, j), lax.bitwise_and(zz, 3)

    def base(step):
        return lax.shift_right_logical(plane(step), 2) * HALF

    barrier = pltpu.get_barrier_semaphore()

    def greet(j):
        _, dev = plane_peer(j)
        pl.semaphore_signal(barrier, inc=1, device_id=dev, device_id_type=MESH_ID)

    each_peer(greet)
    for step, j in [(3, 0), (5, 0), (2, 0), (6, 0)] + [(step, j) for j, _ in CROSS for step in (1, 7)]:
        pl.semaphore_signal(barrier, inc=1, device_id=z_peer(step, j), device_id_type=MESH_ID)

    for load in loads[:2]:
        load.wait()
    values = spec[...].astype(jnp.float32).reshape(F // 2, ROWS, SHARD)
    squares = jnp.sum(values * values, axis=0)
    row = lax.broadcasted_iota(jnp.int32, (ROWS, SHARD), 0)
    first = (row % 4) < 2
    power0 = jnp.sum(jnp.where(first, squares, 0.0), axis=0, keepdims=True) / (2 * F)
    power1 = jnp.sum(jnp.where(first, 0.0, squares), axis=0, keepdims=True) / (2 * F)
    scale = lax.rsqrt(jnp.where(first, power0, power1) + EPSILON)
    keep = (1 - bad_ref[...]).astype(jnp.float32)
    whitened = values * scale[None] * keep[None]
    padded = jnp.concatenate([whitened, jnp.zeros((F // 2, ROWS, TILE - SHARD), jnp.float32)], axis=2)
    padded = padded.astype(jnp.bfloat16)
    white[:, 0] = padded
    for g in range(PLANE // 4):
        white[pl.ds((4 * g) ^ FAR, 4), 1] = padded[4 * g : 4 * g + 4]

    pl.semaphore_wait(barrier, PLANE - 1 + 4 + 2 * len(CROSS))

    pltpu.make_async_copy(white.at[me], mine.at[me], sem_a_recv).start()

    def spread(j):
        k, dev = plane_peer(j)
        pltpu.make_async_remote_copy(
            src_ref=white.at[k], dst_ref=mine.at[me], send_sem=sem_a_send, recv_sem=sem_a_recv,
            device_id=dev, device_id_type=MESH_ID,
        ).start()

    each_peer(spread)

    for load in loads[2:]:
        load.wait()
    pltpu.make_async_copy(tile_ref, tiles_in.at[0], sem_t_recv).start()

    def send_tiles(slot, dev):
        pltpu.make_async_remote_copy(
            src_ref=tile_ref, dst_ref=tiles_in.at[slot], send_sem=sem_t_send, recv_sem=sem_t_recv,
            device_id=dev, device_id_type=MESH_ID,
        ).start()

    for n, j in enumerate(INSIDE[1:], 1):
        send_tiles(n, plane_peer(j)[1])
    for n, (j, dc) in enumerate(CROSS, len(INSIDE)):
        send_tiles(n, z_peer((1, 7)[dc], j))

    out_ref[...] = jnp.zeros_like(out_ref)
    for fine in range(1, FINE):
        column = 2 * (fine - 1)
        cosines[fine - 1] = jnp.broadcast_to(right_table[:, column : column + 1], (DEPTH, TILE))
        sines[fine - 1] = jnp.broadcast_to(right_table[:, column + 1 : column + 2], (DEPTH, TILE))

    pltpu.make_async_copy(mine, mine, sem_a_recv).wait()

    lane = lax.broadcasted_iota(jnp.int32, (ROWS, TILE), 1)
    own = half * HALF

    def to_blocks(kind, dst, start):
        for g in range(PLANE // 4):
            s0, s1, s2, s3 = (mine[4 * g + i, kind].astype(jnp.float32) for i in range(4))
            s1 = pltpu.roll(s1, 96, 1)
            s2 = pltpu.roll(s2, 64, 1)
            s3 = pltpu.roll(s3, 32, 1)
            dst[start + 3 * g] = jnp.where(lane < 96, s0, s1).astype(jnp.bfloat16)
            dst[start + 3 * g + 1] = jnp.where(lane < 64, s1, s2).astype(jnp.bfloat16)
            dst[start + 3 * g + 2] = jnp.where(lane < 32, s2, s3).astype(jnp.bfloat16)

    def send_z(src, dst, chunk, at, count, step):
        pltpu.make_async_remote_copy(
            src_ref=src, dst_ref=dst.at[pl.ds(at, count)],
            send_sem=sem_z_send, recv_sem=sem_z_recv.at[chunk],
            device_id=z_peer(step), device_id_type=MESH_ID,
        ).start()

    to_blocks(odd, zb3, own)
    for step in (2, 6):
        send_z(zb3.at[pl.ds(own, HALF)], zb0, 0, own, HALF, step)
    to_blocks(1 - odd, other, 0)
    for step, chunk in ((7, 1), (3, 1), (1, 2), (5, 2)):
        send_z(other, zbs[chunk], chunk, own, HALF, step)

    pltpu.make_async_copy(tiles_in, tiles_in, sem_t_recv).wait()
    to_smem = pltpu.make_async_copy(tiles_in, tiles, sem_t_local)
    to_smem.start()
    to_smem.wait()

    slot = lax.bitwise_xor(me, odd * FAR)
    wanted = [(plane_peer(j)[1], tm) for j in INSIDE]
    for j, dc in CROSS:
        dev = z_peer((7, 1)[dc], j)
        wanted.append((dev, dev[1]))

    def deliver(chunk, n):
        pltpu.make_async_remote_copy(
            src_ref=pack.at[chunk, n], dst_ref=got.at[chunk, slot],
            send_sem=sem_p_send, recv_sem=sem_p_recv.at[chunk],
            device_id=wanted[n][0], device_id_type=MESH_ID,
        ).start()

    for chunk in range(4):
        zb = zbs[chunk]
        if chunk < 3:
            pltpu.make_async_copy(zb, zb, sem_z_recv.at[chunk]).wait()
        else:
            other = zb.at[pl.ds((1 - half) * HALF, HALF)]
            pltpu.make_async_copy(other, other, sem_z_recv.at[chunk]).wait()
        if chunk == 0:
            for step, at in ((2, base(6)), (6, base(2) + HALF // 2)):
                send_z(zb0.at[pl.ds(at, HALF // 2)], zb3, 3, at, HALF // 2, step)

        if chunk == 1:
            for n in range(len(INSIDE), PLANE):
                deliver(0, n)
        for n in range(0, PLANE, 4):
            places = [(n + u, s) for u in range(4) for s in range(SLOTS)]
            blocks = [zb[tiles[i, s % 2, 2 * wanted[i][1] + s // 2]] for i, s in places]
            for (i, s), block in zip(places, blocks):
                pack[chunk, i, s] = block
        pltpu.make_async_copy(pack.at[chunk, 0], got.at[chunk, slot], sem_p_recv.at[chunk]).start()
        for n in reversed(range(1, len(INSIDE) if chunk == 0 else PLANE)):
            deliver(chunk, n)

    even_lane = lax.broadcasted_iota(jnp.int32, (TILE, TILE), 1) % 2 == 0
    even_row = lax.broadcasted_iota(jnp.int32, (PLANE, ROWS, TILE), 1) % 2 == 0

    def correlate(chunk, carry):
        part = got.at[chunk]
        pltpu.make_async_copy(part, part, sem_p_recv.at[chunk]).wait()

        def one_tile(i, carry):
            a = got[chunk, :, 2 * i].astype(jnp.float32).reshape(DEPTH, TILE)
            for h in range(DEPTH // TILE):
                block = a[h * TILE : (h + 1) * TILE].T
                turned = jnp.where(even_lane, -pltpu.roll(block, TILE - 1, 1), pltpu.roll(block, 1, 1))
                cols = pl.ds(h * TILE, TILE)
                for c in range(COARSE):
                    cos = left_table[2 * c : 2 * c + 1, h * TILE : (h + 1) * TILE]
                    sin = left_table[2 * c + 1 : 2 * c + 2, h * TILE : (h + 1) * TILE]
                    lhs[pl.ds(c * TILE, TILE), cols] = (block * cos + turned * sin).astype(jnp.bfloat16)
            b = got[chunk, :, 2 * i + 1].astype(jnp.float32)
            turned = jnp.where(even_row, pltpu.roll(b, ROWS - 1, 1), -pltpu.roll(b, 1, 1)).reshape(DEPTH, TILE)
            b = b.reshape(DEPTH, TILE)
            rhs[:, 0:TILE] = b.astype(jnp.bfloat16)
            for fine in range(1, FINE):
                rotated = b * cosines[fine - 1] + turned * sines[fine - 1]
                rhs[:, fine * TILE : (fine + 1) * TILE] = rotated.astype(jnp.bfloat16)
            for n in range(2):
                weights = rhs[:, 2 * n * TILE : (2 * n + 2) * TILE]
                for c in range(0, COARSE, 2):
                    res = jnp.dot(lhs[c * TILE : (c + 2) * TILE, :], weights, preferred_element_type=jnp.float32)
                    for dc in range(2):
                        for dn in range(2):
                            lag = FINE * (c + dc) + 2 * n + dn
                            out_ref[i, lag] += res[dc * TILE : (dc + 1) * TILE, dn * TILE : (dn + 1) * TILE]
            return carry

        return lax.fori_loop(0, 2, one_tile, carry)

    lax.fori_loop(0, 4, correlate, 0)

    sent = white.at[pl.ds(0, PLANE - 1)]
    pltpu.make_async_copy(sent, sent, sem_a_send).wait()
    sent = tiles_in.at[pl.ds(0, PLANE - 1)]
    pltpu.make_async_copy(sent, sent, sem_t_send).wait()
    for _ in range(7):
        sent = zb3.at[pl.ds(0, HALF)]
        pltpu.make_async_copy(sent, sent, sem_z_send).wait()
    sent = pack.at[:, pl.ds(0, PLANE - 1)]
    pltpu.make_async_copy(sent, sent, sem_p_send).wait()


def fused(spectra, bad, tile_pairs):
    vmem = pl.BlockSpec(memory_space=pltpu.VMEM)
    slab = pltpu.VMEM((2 * HALF, ROWS, TILE), jnp.bfloat16)
    dma = pltpu.SemaphoreType.DMA
    left_table, right_table = lag_tables()
    return pl.pallas_call(
        fused_kernel,
        out_shape=jax.ShapeDtypeStruct((2, LAGS, TILE, TILE), jnp.float32),
        in_specs=[pl.BlockSpec(memory_space=pltpu.HBM)] * 5,
        out_specs=vmem,
        scratch_shapes=[
            pltpu.VMEM((F * 4, SHARD), jnp.bfloat16),
            pltpu.VMEM((1, SHARD), jnp.int32),
            pltpu.VMEM((2, 8), jnp.int32),
            pltpu.VMEM((2 * COARSE, DEPTH), jnp.float32),
            pltpu.VMEM((DEPTH, TILE), jnp.float32),
            pltpu.VMEM((PLANE, 2, ROWS, TILE), jnp.bfloat16),
            pltpu.VMEM((PLANE, 2, ROWS, TILE), jnp.bfloat16),
            pltpu.VMEM((PLANE, 2, 8), jnp.int32),
            pltpu.SMEM((PLANE, 2, 8), jnp.int32),
            slab, slab, slab, slab,
            pltpu.VMEM((4, PLANE, SLOTS, ROWS, TILE), jnp.bfloat16),
            pltpu.VMEM((4, PLANE, SLOTS, ROWS, TILE), jnp.bfloat16),
            pltpu.VMEM((FINE - 1, DEPTH, TILE), jnp.float32),
            pltpu.VMEM((FINE - 1, DEPTH, TILE), jnp.float32),
            pltpu.VMEM((COARSE * TILE, DEPTH), jnp.bfloat16),
            pltpu.VMEM((DEPTH, FINE * TILE), jnp.bfloat16),
            pltpu.VMEM((HALF, ROWS, TILE), jnp.bfloat16),
            dma((5,)), dma, dma, dma, dma, dma, dma, dma((4,)), dma, dma((4,)),
        ],
        compiler_params=pltpu.CompilerParams(
            collective_id=0, has_side_effects=True, vmem_limit_bytes=16 << 20
        ),
        name="fused",
    )(*(pltpu.with_memory_space_constraint(v, pltpu.HBM) for v in (spectra, bad, tile_pairs, jnp.asarray(left_table), jnp.asarray(right_table))))


def lag_tables():
    row = np.arange(DEPTH)
    bin_number = 2 * (row // ROWS) + (row % ROWS) // 4 + 1.0
    angle = np.pi / F * bin_number
    coarse = FINE * np.arange(COARSE) - LAGS // 2
    norm = 1.0 / math.sqrt(F * HOURS)
    left = np.stack([np.cos(coarse[:, None] * angle), np.sin(coarse[:, None] * angle)], axis=1) * norm
    right = np.zeros((DEPTH, TILE))
    for fine in range(1, FINE):
        right[:, 2 * fine - 2] = np.cos(fine * angle)
        right[:, 2 * fine - 1] = np.sin(fine * angle)
    return left.reshape(2 * COARSE, DEPTH).astype(np.float32), right.astype(np.float32)


def per_device(spectra, bad_channels, tile_list):
    rows = spectra.reshape(F * 4, SHARD)
    return fused(rows, bad_channels.reshape(1, SHARD), tile_list.T)


def solution(mesh):
    placed = (P(None, "tm", None, "chan"), P("chan"), P("chan", None))
    return jax.shard_map(
        per_device,
        mesh=mesh,
        in_specs=placed,
        out_specs=P(("chan", "tm"), None, None, None),
        check_vma=False,
    )
```

```python
import math

import jax
import jax.numpy as jnp
import numpy as np
from jax import lax
from jax.experimental import pallas as pl
from jax.experimental.pallas import tpu as pltpu
from jax.sharding import PartitionSpec as P

F = 64
HOURS = 8
LAGS = 32
TILE = 128
EPSILON = 1e-06

PLANE = 32
SHARD = 96
HALF = 24
ROWS = 8
DEPTH = PLANE * ROWS
SLOTS = 4
FINE = 4
COARSE = LAGS // FINE
FAR = 20
NEAR = (0, 2, 6, 8, 24)
CROSS = tuple((near + dc, dc) for near in NEAR for dc in range(2))
INSIDE = tuple(j for j in range(PLANE) if (j & ~1) ^ FAR not in NEAR)
MESH_ID = pl.DeviceIdType.MESH


def load_blocks(got, i, left_table, cosines, sines, lhs, rhs):
    even_lane = lax.broadcasted_iota(jnp.int32, (TILE, TILE), 1) % 2 == 0
    even_row = lax.broadcasted_iota(jnp.int32, (PLANE, ROWS, TILE), 1) % 2 == 0
    a = got[:, 2 * i].astype(jnp.float32).reshape(DEPTH, TILE)
    for h in range(DEPTH // TILE):
        block = a[h * TILE : (h + 1) * TILE].T
        turned = jnp.where(even_lane, -pltpu.roll(block, TILE - 1, 1), pltpu.roll(block, 1, 1))
        cols = pl.ds(h * TILE, TILE)
        for c in range(COARSE):
            cos = left_table[2 * c : 2 * c + 1, h * TILE : (h + 1) * TILE]
            sin = left_table[2 * c + 1 : 2 * c + 2, h * TILE : (h + 1) * TILE]
            lhs[pl.ds(c * TILE, TILE), cols] = (block * cos + turned * sin).astype(jnp.bfloat16)
    b = got[:, 2 * i + 1].astype(jnp.float32)
    turned = jnp.where(even_row, pltpu.roll(b, ROWS - 1, 1), -pltpu.roll(b, 1, 1)).reshape(DEPTH, TILE)
    b = b.reshape(DEPTH, TILE)
    rhs[:, 0:TILE] = b.astype(jnp.bfloat16)
    for fine in range(1, FINE):
        rotated = b * cosines[fine - 1] + turned * sines[fine - 1]
        rhs[:, fine * TILE : (fine + 1) * TILE] = rotated.astype(jnp.bfloat16)


def lag_products(lhs, rhs, c, add):
    for n in range(2):
        weights = rhs[:, 2 * n * TILE : (2 * n + 2) * TILE]
        res = jnp.dot(lhs[c * TILE : (c + 2) * TILE, :], weights, preferred_element_type=jnp.float32)
        for dc in range(2):
            for dn in range(2):
                lag = FINE * (c + dc) + 2 * n + dn
                add(lag, res[dc * TILE : (dc + 1) * TILE, dn * TILE : (dn + 1) * TILE])


def finish_kernel(last, partial, left_table, cosines, sines, out_hbm, stage, lhs, rhs, sems):
    copies = []
    for i in range(2):
        load_blocks(last, i, left_table, cosines, sines, lhs.at[i], rhs.at[i])
        for c in range(0, COARSE, 2):
            def put(lag, value):
                stage[i, lag] = partial[i, lag] + value

            lag_products(lhs.at[i], rhs.at[i], c, put)
            lags = pl.ds(FINE * c, 2 * FINE)
            copies.append(pltpu.make_async_copy(stage.at[i, lags], out_hbm.at[i, lags], sems.at[len(copies)]))
            copies[-1].start()
    for copy in copies:
        copy.wait()


def fused_kernel(
    spec_hbm, bad_hbm, tile_hbm, left_hbm, right_hbm, out_ref, last, left_table, cosines, sines,
    spec, bad_ref, tile_ref, right_table, white, mine, mine_other, tiles_in, tiles, zb0, zb1, zb2, zb3, pack, got, lhs, rhs, other,
    sem_in, sem_a_send, sem_a_recv, sem_b_recv, sem_t_send, sem_t_recv, sem_t_local, sem_z_send, sem_z_recv,
    sem_p_send, sem_p_recv,
):
    zbs = (zb0, zb1, zb2, zb3)
    chan, tm = lax.axis_index("chan"), lax.axis_index("tm")
    half = lax.shift_right_logical(chan, 5)
    me = lax.bitwise_and(chan, PLANE - 1)
    z = half * 4 + tm
    odd = lax.bitwise_and(z, 1)

    loads = [
        pltpu.make_async_copy(src, dst, sem_in.at[i])
        for i, (src, dst) in enumerate(
            ((spec_hbm, spec), (bad_hbm, bad_ref), (tile_hbm, tile_ref), (left_hbm, left_table), (right_hbm, right_table))
        )
    ]
    for load in loads:
        load.start()

    def plane_peer(j):
        k = lax.bitwise_xor(me, j)
        return k, (lax.bitwise_xor(chan, j), tm)

    def each_peer(act):
        def four(i, carry):
            for u in range(4):
                act(lax.bitwise_xor(4 * i + u, FAR))
            return carry

        lax.fori_loop(0, FAR // 4, four, 0)
        for u in range(FAR + 1, FAR + 4):
            act(u ^ FAR)
        lax.fori_loop(FAR // 4 + 1, PLANE // 4, four, 0)

    def plane(step):
        return lax.bitwise_and(z + step, 7)

    def z_peer(step, j=0):
        zz = plane(step)
        return lax.shift_right_logical(zz, 2) * PLANE + lax.bitwise_xor(me, j), lax.bitwise_and(zz, 3)

    def base(step):
        return lax.shift_right_logical(plane(step), 2) * HALF

    barrier = pltpu.get_barrier_semaphore()

    def greet(j):
        _, dev = plane_peer(j)
        pl.semaphore_signal(barrier, inc=1, device_id=dev, device_id_type=MESH_ID)

    each_peer(greet)
    for step, j in [(3, 0), (5, 0), (2, 0), (6, 0)] + [(step, j) for j, _ in CROSS for step in (1, 7)]:
        pl.semaphore_signal(barrier, inc=1, device_id=z_peer(step, j), device_id_type=MESH_ID)

    for load in loads[:2]:
        load.wait()
    values = spec[...].astype(jnp.float32).reshape(F // 2, ROWS, SHARD)
    squares = jnp.sum(values * values, axis=0)
    row = lax.broadcasted_iota(jnp.int32, (ROWS, SHARD), 0)
    first = (row % 4) < 2
    power0 = jnp.sum(jnp.where(first, squares, 0.0), axis=0, keepdims=True) / (2 * F)
    power1 = jnp.sum(jnp.where(first, 0.0, squares), axis=0, keepdims=True) / (2 * F)
    scale = lax.rsqrt(jnp.where(first, power0, power1) + EPSILON)
    keep = (1 - bad_ref[...]).astype(jnp.float32)
    whitened = values * scale[None] * keep[None]
    padded = jnp.concatenate([whitened, jnp.zeros((F // 2, ROWS, TILE - SHARD), jnp.float32)], axis=2)
    padded = padded.astype(jnp.bfloat16)
    white[...] = padded

    pl.semaphore_wait(barrier, PLANE - 1 + 4 + 2 * len(CROSS))

    for kind, dst, sem in ((odd, mine, sem_a_recv), (1 - odd, mine_other, sem_b_recv)):
        shift = kind * FAR
        pltpu.make_async_copy(white.at[lax.bitwise_xor(me, shift)], dst.at[me], sem).start()

        def spread(j):
            k, dev = plane_peer(j)
            pltpu.make_async_remote_copy(
                src_ref=white.at[lax.bitwise_xor(k, shift)], dst_ref=dst.at[me], send_sem=sem_a_send, recv_sem=sem,
                device_id=dev, device_id_type=MESH_ID,
            ).start()

        each_peer(spread)

    for load in loads[2:]:
        load.wait()
    pltpu.make_async_copy(tile_ref, tiles_in.at[0], sem_t_recv).start()

    def send_tiles(slot, dev):
        pltpu.make_async_remote_copy(
            src_ref=tile_ref, dst_ref=tiles_in.at[slot], send_sem=sem_t_send, recv_sem=sem_t_recv,
            device_id=dev, device_id_type=MESH_ID,
        ).start()

    for n, j in enumerate(INSIDE[1:], 1):
        send_tiles(n, plane_peer(j)[1])
    for n, (j, dc) in enumerate(CROSS, len(INSIDE)):
        send_tiles(n, z_peer((1, 7)[dc], j))

    out_ref[...] = jnp.zeros_like(out_ref)
    for fine in range(1, FINE):
        column = 2 * (fine - 1)
        cosines[fine - 1] = jnp.broadcast_to(right_table[:, column : column + 1], (DEPTH, TILE))
        sines[fine - 1] = jnp.broadcast_to(right_table[:, column + 1 : column + 2], (DEPTH, TILE))

    lane = lax.broadcasted_iota(jnp.int32, (ROWS, TILE), 1)
    own = half * HALF

    def to_blocks(src, dst, start):
        for g in range(PLANE // 4):
            s0, s1, s2, s3 = (src[4 * g + i].astype(jnp.float32) for i in range(4))
            s1 = pltpu.roll(s1, 96, 1)
            s2 = pltpu.roll(s2, 64, 1)
            s3 = pltpu.roll(s3, 32, 1)
            dst[start + 3 * g] = jnp.where(lane < 96, s0, s1).astype(jnp.bfloat16)
            dst[start + 3 * g + 1] = jnp.where(lane < 64, s1, s2).astype(jnp.bfloat16)
            dst[start + 3 * g + 2] = jnp.where(lane < 32, s2, s3).astype(jnp.bfloat16)

    def send_z(src, dst, chunk, at, count, step):
        pltpu.make_async_remote_copy(
            src_ref=src, dst_ref=dst.at[pl.ds(at, count)],
            send_sem=sem_z_send, recv_sem=sem_z_recv.at[chunk],
            device_id=z_peer(step), device_id_type=MESH_ID,
        ).start()

    pltpu.make_async_copy(mine, mine, sem_a_recv).wait()
    to_blocks(mine, zb3, own)
    for step in (2, 6):
        send_z(zb3.at[pl.ds(own, HALF)], zb0, 0, own, HALF, step)
    pltpu.make_async_copy(mine_other, mine_other, sem_b_recv).wait()
    to_blocks(mine_other, other, 0)
    for step, chunk in ((7, 1), (3, 1), (1, 2), (5, 2)):
        send_z(other, zbs[chunk], chunk, own, HALF, step)

    pltpu.make_async_copy(tiles_in, tiles_in, sem_t_recv).wait()
    to_smem = pltpu.make_async_copy(tiles_in, tiles, sem_t_local)
    to_smem.start()
    to_smem.wait()

    slot = lax.bitwise_xor(me, odd * FAR)
    wanted = [(plane_peer(j)[1], tm) for j in INSIDE]
    for j, dc in CROSS:
        dev = z_peer((7, 1)[dc], j)
        wanted.append((dev, dev[1]))

    def landing(chunk):
        return got.at[chunk, slot] if chunk < 3 else last.at[slot]

    def deliver(chunk, n):
        pltpu.make_async_remote_copy(
            src_ref=pack.at[chunk, n], dst_ref=landing(chunk),
            send_sem=sem_p_send, recv_sem=sem_p_recv.at[chunk],
            device_id=wanted[n][0], device_id_type=MESH_ID,
        ).start()

    for chunk in range(4):
        zb = zbs[chunk]
        late = zb if chunk < 3 else zb.at[pl.ds(base(4), HALF)]
        pltpu.make_async_copy(late, late, sem_z_recv.at[chunk]).wait()
        if chunk == 0:
            for step, at in ((2, base(6)), (6, base(2) + HALF // 2)):
                send_z(zb0.at[pl.ds(at, HALF // 2)], zb3, 3, at, HALF // 2, step)

        if chunk == 1:
            for n in range(len(INSIDE), PLANE):
                deliver(0, n)
        for n in range(0, PLANE, 4):
            places = [(n + u, s) for u in range(4) for s in range(SLOTS)]
            blocks = [zb[tiles[i, s % 2, 2 * wanted[i][1] + s // 2]] for i, s in places]
            for (i, s), block in zip(places, blocks):
                pack[chunk, i, s] = block
        pltpu.make_async_copy(pack.at[chunk, 0], landing(chunk), sem_p_recv.at[chunk]).start()
        for n in reversed(range(1, len(INSIDE) if chunk == 0 else PLANE)):
            deliver(chunk, n)

    def correlate(chunk, carry):
        part = got.at[chunk]
        pltpu.make_async_copy(part, part, sem_p_recv.at[chunk]).wait()

        def one_tile(i, carry):
            def add(lag, value):
                out_ref[i, lag] += value

            load_blocks(part, i, left_table, cosines, sines, lhs, rhs)
            for c in range(0, COARSE, 2):
                lag_products(lhs, rhs, c, add)
            return carry

        return lax.fori_loop(0, 2, one_tile, carry)

    lax.fori_loop(0, 3, correlate, 0)

    pltpu.make_async_copy(last, last, sem_p_recv.at[3]).wait()
    sent = white.at[pl.ds(0, PLANE - 1)]
    for _ in range(2):
        pltpu.make_async_copy(sent, sent, sem_a_send).wait()
    sent = tiles_in.at[pl.ds(0, PLANE - 1)]
    pltpu.make_async_copy(sent, sent, sem_t_send).wait()
    for _ in range(7):
        sent = zb3.at[pl.ds(0, HALF)]
        pltpu.make_async_copy(sent, sent, sem_z_send).wait()
    sent = pack.at[:, pl.ds(0, PLANE - 1)]
    pltpu.make_async_copy(sent, sent, sem_p_send).wait()


def fused(spectra, bad, tile_pairs):
    vmem = pl.BlockSpec(memory_space=pltpu.VMEM)
    slab = pltpu.VMEM((2 * HALF, ROWS, TILE), jnp.bfloat16)
    dma = pltpu.SemaphoreType.DMA
    left_table, right_table = lag_tables()
    block = (PLANE, SLOTS, ROWS, TILE)
    table = (FINE - 1, DEPTH, TILE)
    partial, *rest = pl.pallas_call(
        fused_kernel,
        out_shape=[
            jax.ShapeDtypeStruct((2, LAGS, TILE, TILE), jnp.float32),
            jax.ShapeDtypeStruct(block, jnp.bfloat16),
            jax.ShapeDtypeStruct((2 * COARSE, DEPTH), jnp.float32),
            jax.ShapeDtypeStruct(table, jnp.float32),
            jax.ShapeDtypeStruct(table, jnp.float32),
        ],
        in_specs=[pl.BlockSpec(memory_space=pltpu.HBM)] * 5,
        out_specs=[vmem] * 5,
        scratch_shapes=[
            pltpu.VMEM((F * 4, SHARD), jnp.bfloat16),
            pltpu.VMEM((1, SHARD), jnp.int32),
            pltpu.VMEM((2, 8), jnp.int32),
            pltpu.VMEM((DEPTH, TILE), jnp.float32),
            pltpu.VMEM((PLANE, ROWS, TILE), jnp.bfloat16),
            pltpu.VMEM((PLANE, ROWS, TILE), jnp.bfloat16),
            pltpu.VMEM((PLANE, ROWS, TILE), jnp.bfloat16),
            pltpu.VMEM((PLANE, 2, 8), jnp.int32),
            pltpu.SMEM((PLANE, 2, 8), jnp.int32),
            slab, slab, slab, slab,
            pltpu.VMEM((4, *block), jnp.bfloat16),
            pltpu.VMEM((3, *block), jnp.bfloat16),
            pltpu.VMEM((COARSE * TILE, DEPTH), jnp.bfloat16),
            pltpu.VMEM((DEPTH, FINE * TILE), jnp.bfloat16),
            pltpu.VMEM((HALF, ROWS, TILE), jnp.bfloat16),
            dma((5,)), dma, dma, dma, dma, dma, dma, dma, dma((4,)), dma, dma((4,)),
        ],
        compiler_params=pltpu.CompilerParams(
            collective_id=0, has_side_effects=True, vmem_limit_bytes=16 << 20
        ),
        name="fused",
    )(*(
        pltpu.with_memory_space_constraint(v, pltpu.HBM)
        for v in (spectra, bad, tile_pairs, jnp.asarray(left_table), jnp.asarray(right_table))
    ))
    return pl.pallas_call(
        finish_kernel,
        out_shape=jax.ShapeDtypeStruct((2, LAGS, TILE, TILE), jnp.float32),
        in_specs=[vmem] * 5,
        out_specs=pl.BlockSpec(memory_space=pltpu.HBM),
        scratch_shapes=[
            pltpu.VMEM((2, LAGS, TILE, TILE), jnp.float32),
            pltpu.VMEM((2, COARSE * TILE, DEPTH), jnp.bfloat16),
            pltpu.VMEM((2, DEPTH, FINE * TILE), jnp.bfloat16),
            dma((COARSE,)),
        ],
        compiler_params=pltpu.CompilerParams(vmem_limit_bytes=12 << 20),
        name="finish",
    )(rest[0], partial, *rest[1:])


def lag_tables():
    row = np.arange(DEPTH)
    bin_number = 2 * (row // ROWS) + (row % ROWS) // 4 + 1.0
    angle = np.pi / F * bin_number
    coarse = FINE * np.arange(COARSE) - LAGS // 2
    norm = 1.0 / math.sqrt(F * HOURS)
    left = np.stack([np.cos(coarse[:, None] * angle), np.sin(coarse[:, None] * angle)], axis=1) * norm
    right = np.zeros((DEPTH, TILE))
    for fine in range(1, FINE):
        right[:, 2 * fine - 2] = np.cos(fine * angle)
        right[:, 2 * fine - 1] = np.sin(fine * angle)
    return left.reshape(2 * COARSE, DEPTH).astype(np.float32), right.astype(np.float32)


def per_device(spectra, bad_channels, tile_list):
    rows = spectra.reshape(F * 4, SHARD)
    return fused(rows, bad_channels.reshape(1, SHARD), tile_list.T)


def solution(mesh):
    placed = (P(None, "tm", None, "chan"), P("chan"), P("chan", None))
    return jax.shard_map(
        per_device,
        mesh=mesh,
        in_specs=placed,
        out_specs=P(("chan", "tm"), None, None, None),
        check_vma=False,
    )
```

```python
import math

import jax
import jax.numpy as jnp
import numpy as np
from jax import lax
from jax.experimental import pallas as pl
from jax.experimental.pallas import tpu as pltpu
from jax.sharding import PartitionSpec as P

F = 64
HOURS = 8
LAGS = 32
TILE = 128
EPSILON = 1e-06

PLANE = 32
SHARD = 96
HALF = 24
ROWS = 8
DEPTH = PLANE * ROWS
SLOTS = 4
FINE = 4
COARSE = LAGS // FINE
FAR = 20
NEAR = (0, 2, 6, 8, 24)
CROSS = tuple((near + dc, dc) for near in NEAR for dc in range(2))
INSIDE = tuple(j for j in range(PLANE) if (j & ~1) ^ FAR not in NEAR)
MESH_ID = pl.DeviceIdType.MESH


def load_blocks(got, i, left_table, cosines, sines, swap, eye, lhs, rhs):
    a = got[:, 2 * i].astype(jnp.float32).reshape(DEPTH, TILE).astype(jnp.bfloat16)
    a = lax.dot_general(eye[...], a, (((1,), (1,)), ((), ())), preferred_element_type=jnp.float32)
    turned = jnp.dot(a.astype(jnp.bfloat16), swap[...], preferred_element_type=jnp.float32)
    for c in range(COARSE):
        rotated = a * left_table[2 * c : 2 * c + 1] + turned * left_table[2 * c + 1 : 2 * c + 2]
        lhs[pl.ds(c * TILE, TILE)] = rotated.astype(jnp.bfloat16)
    b = got[:, 2 * i + 1].astype(jnp.float32).reshape(DEPTH, TILE)
    exact = b.astype(jnp.bfloat16)
    turned = jnp.dot(swap[...], exact, preferred_element_type=jnp.float32)
    rhs[:, 0:TILE] = exact
    for fine in range(1, FINE):
        rotated = b * cosines[fine - 1] + turned * sines[fine - 1]
        rhs[:, fine * TILE : (fine + 1) * TILE] = rotated.astype(jnp.bfloat16)


def lag_products(lhs, rhs, c, add):
    for n in range(2):
        weights = rhs[:, 2 * n * TILE : (2 * n + 2) * TILE]
        res = jnp.dot(lhs[c * TILE : (c + 2) * TILE, :], weights, preferred_element_type=jnp.float32)
        for dc in range(2):
            for dn in range(2):
                lag = FINE * (c + dc) + 2 * n + dn
                add(lag, res[dc * TILE : (dc + 1) * TILE, dn * TILE : (dn + 1) * TILE])


def finish_kernel(last, partial, left_table, cosines, sines, swap, eye, out_hbm, stage, lhs, rhs, sems):
    copies = []
    for i in range(2):
        load_blocks(last, i, left_table, cosines, sines, swap, eye, lhs.at[i], rhs.at[i])
        for c in range(0, COARSE, 2):
            def put(lag, value):
                stage[i, lag] = partial[i, lag] + value

            lag_products(lhs.at[i], rhs.at[i], c, put)
            lags = pl.ds(FINE * c, 2 * FINE)
            copies.append(pltpu.make_async_copy(stage.at[i, lags], out_hbm.at[i, lags], sems.at[len(copies)]))
            copies[-1].start()
    for copy in copies:
        copy.wait()


def fused_kernel(
    spec_hbm, bad_hbm, tile_hbm, left_hbm, right_hbm, out_ref, last, left_table, cosines, sines, swap, eye,
    spec, bad_ref, tile_ref, right_table, white, mine, mine_other, tiles_in, tiles, zb0, zb1, zb2, zb3, pack, got, lhs, rhs, other,
    sem_in, sem_a_send, sem_a_recv, sem_b_recv, sem_t_send, sem_t_recv, sem_t_local, sem_z_send, sem_z_recv,
    sem_p_send, sem_p_recv,
):
    zbs = (zb0, zb1, zb2, zb3)
    chan, tm = lax.axis_index("chan"), lax.axis_index("tm")
    half = lax.shift_right_logical(chan, 5)
    me = lax.bitwise_and(chan, PLANE - 1)
    z = half * 4 + tm
    odd = lax.bitwise_and(z, 1)

    loads = [
        pltpu.make_async_copy(src, dst, sem_in.at[i])
        for i, (src, dst) in enumerate(
            ((spec_hbm, spec), (bad_hbm, bad_ref), (tile_hbm, tile_ref), (left_hbm, left_table), (right_hbm, right_table))
        )
    ]
    for load in loads:
        load.start()

    def plane_peer(j):
        k = lax.bitwise_xor(me, j)
        return k, (lax.bitwise_xor(chan, j), tm)

    def each_peer(act):
        def four(i, carry):
            for u in range(4):
                act(lax.bitwise_xor(4 * i + u, FAR))
            return carry

        lax.fori_loop(0, FAR // 4, four, 0)
        for u in range(FAR + 1, FAR + 4):
            act(u ^ FAR)
        lax.fori_loop(FAR // 4 + 1, PLANE // 4, four, 0)

    def plane(step):
        return lax.bitwise_and(z + step, 7)

    def z_peer(step, j=0):
        zz = plane(step)
        return lax.shift_right_logical(zz, 2) * PLANE + lax.bitwise_xor(me, j), lax.bitwise_and(zz, 3)

    def base(step):
        return lax.shift_right_logical(plane(step), 2) * HALF

    barrier = pltpu.get_barrier_semaphore()

    def greet(j):
        _, dev = plane_peer(j)
        pl.semaphore_signal(barrier, inc=1, device_id=dev, device_id_type=MESH_ID)

    each_peer(greet)
    for step, j in [(3, 0), (5, 0), (2, 0), (6, 0)] + [(step, j) for j, _ in CROSS for step in (1, 7)]:
        pl.semaphore_signal(barrier, inc=1, device_id=z_peer(step, j), device_id_type=MESH_ID)

    for load in loads[:2]:
        load.wait()
    values = spec[...].astype(jnp.float32).reshape(F // 2, ROWS, SHARD)
    squares = jnp.sum(values * values, axis=0)
    row = lax.broadcasted_iota(jnp.int32, (ROWS, SHARD), 0)
    first = (row % 4) < 2
    power0 = jnp.sum(jnp.where(first, squares, 0.0), axis=0, keepdims=True) / (2 * F)
    power1 = jnp.sum(jnp.where(first, 0.0, squares), axis=0, keepdims=True) / (2 * F)
    scale = lax.rsqrt(jnp.where(first, power0, power1) + EPSILON)
    keep = (1 - bad_ref[...]).astype(jnp.float32)
    whitened = values * scale[None] * keep[None]
    padded = jnp.concatenate([whitened, jnp.zeros((F // 2, ROWS, TILE - SHARD), jnp.float32)], axis=2)
    padded = padded.astype(jnp.bfloat16)
    white[...] = padded

    pl.semaphore_wait(barrier, PLANE - 1 + 4 + 2 * len(CROSS))

    for kind, dst, sem in ((odd, mine, sem_a_recv), (1 - odd, mine_other, sem_b_recv)):
        shift = kind * FAR
        pltpu.make_async_copy(white.at[lax.bitwise_xor(me, shift)], dst.at[me], sem).start()

        def spread(j):
            k, dev = plane_peer(j)
            pltpu.make_async_remote_copy(
                src_ref=white.at[lax.bitwise_xor(k, shift)], dst_ref=dst.at[me], send_sem=sem_a_send, recv_sem=sem,
                device_id=dev, device_id_type=MESH_ID,
            ).start()

        each_peer(spread)

    for load in loads[2:]:
        load.wait()
    pltpu.make_async_copy(tile_ref, tiles_in.at[0], sem_t_recv).start()

    def send_tiles(slot, dev):
        pltpu.make_async_remote_copy(
            src_ref=tile_ref, dst_ref=tiles_in.at[slot], send_sem=sem_t_send, recv_sem=sem_t_recv,
            device_id=dev, device_id_type=MESH_ID,
        ).start()

    for n, j in enumerate(INSIDE[1:], 1):
        send_tiles(n, plane_peer(j)[1])
    for n, (j, dc) in enumerate(CROSS, len(INSIDE)):
        send_tiles(n, z_peer((1, 7)[dc], j))

    out_ref[...] = jnp.zeros_like(out_ref)
    row = lax.broadcasted_iota(jnp.int32, (DEPTH, DEPTH), 0)
    ahead = lax.broadcasted_iota(jnp.int32, (DEPTH, DEPTH), 1) - row
    even = lax.bitwise_and(row, 1) == 0
    to_re = jnp.where(even, jnp.where(ahead == 1, 1.0, 0.0), jnp.where(ahead == -1, -1.0, 0.0))
    swap[...] = to_re.astype(jnp.bfloat16)
    eye[...] = jnp.where(ahead[:TILE, :TILE] == 0, 1.0, 0.0).astype(jnp.bfloat16)
    for fine in range(1, FINE):
        column = 2 * (fine - 1)
        cosines[fine - 1] = jnp.broadcast_to(right_table[:, column : column + 1], (DEPTH, TILE))
        sines[fine - 1] = jnp.broadcast_to(right_table[:, column + 1 : column + 2], (DEPTH, TILE))

    lane = lax.broadcasted_iota(jnp.int32, (ROWS, TILE), 1)
    own = half * HALF

    def to_blocks(src, dst, start):
        for g in range(PLANE // 4):
            s0, s1, s2, s3 = (src[4 * g + i].astype(jnp.float32) for i in range(4))
            s1 = pltpu.roll(s1, 96, 1)
            s2 = pltpu.roll(s2, 64, 1)
            s3 = pltpu.roll(s3, 32, 1)
            dst[start + 3 * g] = jnp.where(lane < 96, s0, s1).astype(jnp.bfloat16)
            dst[start + 3 * g + 1] = jnp.where(lane < 64, s1, s2).astype(jnp.bfloat16)
            dst[start + 3 * g + 2] = jnp.where(lane < 32, s2, s3).astype(jnp.bfloat16)

    def send_z(src, dst, chunk, at, count, step):
        pltpu.make_async_remote_copy(
            src_ref=src, dst_ref=dst.at[pl.ds(at, count)],
            send_sem=sem_z_send, recv_sem=sem_z_recv.at[chunk],
            device_id=z_peer(step), device_id_type=MESH_ID,
        ).start()

    pltpu.make_async_copy(mine, mine, sem_a_recv).wait()
    to_blocks(mine, zb3, own)
    for step in (2, 6):
        send_z(zb3.at[pl.ds(own, HALF)], zb0, 0, own, HALF, step)
    pltpu.make_async_copy(mine_other, mine_other, sem_b_recv).wait()
    to_blocks(mine_other, other, 0)
    for step, chunk in ((7, 1), (3, 1), (1, 2), (5, 2)):
        send_z(other, zbs[chunk], chunk, own, HALF, step)

    pltpu.make_async_copy(tiles_in, tiles_in, sem_t_recv).wait()
    to_smem = pltpu.make_async_copy(tiles_in, tiles, sem_t_local)
    to_smem.start()
    to_smem.wait()

    slot = lax.bitwise_xor(me, odd * FAR)
    wanted = [(plane_peer(j)[1], tm) for j in INSIDE]
    for j, dc in CROSS:
        dev = z_peer((7, 1)[dc], j)
        wanted.append((dev, dev[1]))

    def landing(chunk):
        return got.at[chunk, slot] if chunk < 3 else last.at[slot]

    def deliver(chunk, n):
        pltpu.make_async_remote_copy(
            src_ref=pack.at[chunk, n], dst_ref=landing(chunk),
            send_sem=sem_p_send, recv_sem=sem_p_recv.at[chunk],
            device_id=wanted[n][0], device_id_type=MESH_ID,
        ).start()

    for chunk in range(4):
        zb = zbs[chunk]
        late = zb if chunk < 3 else zb.at[pl.ds(base(4), HALF)]
        pltpu.make_async_copy(late, late, sem_z_recv.at[chunk]).wait()
        if chunk == 0:
            for step, at in ((2, base(6)), (6, base(2) + HALF // 2)):
                send_z(zb0.at[pl.ds(at, HALF // 2)], zb3, 3, at, HALF // 2, step)

        if chunk == 1:
            for n in range(len(INSIDE), PLANE):
                deliver(0, n)
        for n in range(0, PLANE, 4):
            places = [(n + u, s) for u in range(4) for s in range(SLOTS)]
            blocks = [zb[tiles[i, s % 2, 2 * wanted[i][1] + s // 2]] for i, s in places]
            for (i, s), block in zip(places, blocks):
                pack[chunk, i, s] = block
        pltpu.make_async_copy(pack.at[chunk, 0], landing(chunk), sem_p_recv.at[chunk]).start()
        for n in reversed(range(1, len(INSIDE) if chunk == 0 else PLANE)):
            deliver(chunk, n)

    def correlate(chunk, carry):
        part = got.at[chunk]
        pltpu.make_async_copy(part, part, sem_p_recv.at[chunk]).wait()

        def one_tile(i, carry):
            def add(lag, value):
                out_ref[i, lag] += value

            load_blocks(part, i, left_table, cosines, sines, swap, eye, lhs, rhs)
            for c in range(0, COARSE, 2):
                lag_products(lhs, rhs, c, add)
            return carry

        return lax.fori_loop(0, 2, one_tile, carry)

    lax.fori_loop(0, 3, correlate, 0)

    pltpu.make_async_copy(last, last, sem_p_recv.at[3]).wait()
    sent = white.at[pl.ds(0, PLANE - 1)]
    for _ in range(2):
        pltpu.make_async_copy(sent, sent, sem_a_send).wait()
    sent = tiles_in.at[pl.ds(0, PLANE - 1)]
    pltpu.make_async_copy(sent, sent, sem_t_send).wait()
    for _ in range(7):
        sent = zb3.at[pl.ds(0, HALF)]
        pltpu.make_async_copy(sent, sent, sem_z_send).wait()
    sent = pack.at[:, pl.ds(0, PLANE - 1)]
    pltpu.make_async_copy(sent, sent, sem_p_send).wait()


def fused(spectra, bad, tile_pairs):
    vmem = pl.BlockSpec(memory_space=pltpu.VMEM)
    slab = pltpu.VMEM((2 * HALF, ROWS, TILE), jnp.bfloat16)
    dma = pltpu.SemaphoreType.DMA
    left_table, right_table = lag_tables()
    block = (PLANE, SLOTS, ROWS, TILE)
    table = (FINE - 1, DEPTH, TILE)
    partial, *rest = pl.pallas_call(
        fused_kernel,
        out_shape=[
            jax.ShapeDtypeStruct((2, LAGS, TILE, TILE), jnp.float32),
            jax.ShapeDtypeStruct(block, jnp.bfloat16),
            jax.ShapeDtypeStruct((2 * COARSE, DEPTH), jnp.float32),
            jax.ShapeDtypeStruct(table, jnp.float32),
            jax.ShapeDtypeStruct(table, jnp.float32),
            jax.ShapeDtypeStruct((DEPTH, DEPTH), jnp.bfloat16),
            jax.ShapeDtypeStruct((TILE, TILE), jnp.bfloat16),
        ],
        in_specs=[pl.BlockSpec(memory_space=pltpu.HBM)] * 5,
        out_specs=[vmem] * 7,
        scratch_shapes=[
            pltpu.VMEM((F * 4, SHARD), jnp.bfloat16),
            pltpu.VMEM((1, SHARD), jnp.int32),
            pltpu.VMEM((2, 8), jnp.int32),
            pltpu.VMEM((DEPTH, TILE), jnp.float32),
            pltpu.VMEM((PLANE, ROWS, TILE), jnp.bfloat16),
            pltpu.VMEM((PLANE, ROWS, TILE), jnp.bfloat16),
            pltpu.VMEM((PLANE, ROWS, TILE), jnp.bfloat16),
            pltpu.VMEM((PLANE, 2, 8), jnp.int32),
            pltpu.SMEM((PLANE, 2, 8), jnp.int32),
            slab, slab, slab, slab,
            pltpu.VMEM((4, *block), jnp.bfloat16),
            pltpu.VMEM((3, *block), jnp.bfloat16),
            pltpu.VMEM((COARSE * TILE, DEPTH), jnp.bfloat16),
            pltpu.VMEM((DEPTH, FINE * TILE), jnp.bfloat16),
            pltpu.VMEM((HALF, ROWS, TILE), jnp.bfloat16),
            dma((5,)), dma, dma, dma, dma, dma, dma, dma, dma((4,)), dma, dma((4,)),
        ],
        compiler_params=pltpu.CompilerParams(
            collective_id=0, has_side_effects=True, vmem_limit_bytes=16 << 20
        ),
        name="fused",
    )(*(
        pltpu.with_memory_space_constraint(v, pltpu.HBM)
        for v in (spectra, bad, tile_pairs, jnp.asarray(left_table), jnp.asarray(right_table))
    ))
    return pl.pallas_call(
        finish_kernel,
        out_shape=jax.ShapeDtypeStruct((2, LAGS, TILE, TILE), jnp.float32),
        in_specs=[vmem] * 7,
        out_specs=pl.BlockSpec(memory_space=pltpu.HBM),
        scratch_shapes=[
            pltpu.VMEM((2, LAGS, TILE, TILE), jnp.float32),
            pltpu.VMEM((2, COARSE * TILE, DEPTH), jnp.bfloat16),
            pltpu.VMEM((2, DEPTH, FINE * TILE), jnp.bfloat16),
            dma((COARSE,)),
        ],
        compiler_params=pltpu.CompilerParams(vmem_limit_bytes=12 << 20),
        name="finish",
    )(rest[0], partial, *rest[1:])


def lag_tables():
    row = np.arange(DEPTH)
    bin_number = 2 * (row // ROWS) + (row % ROWS) // 4 + 1.0
    angle = np.pi / F * bin_number
    coarse = FINE * np.arange(COARSE) - LAGS // 2
    norm = 1.0 / math.sqrt(F * HOURS)
    left = np.stack([np.cos(coarse[:, None] * angle), np.sin(coarse[:, None] * angle)], axis=1) * norm
    right = np.zeros((DEPTH, TILE))
    for fine in range(1, FINE):
        right[:, 2 * fine - 2] = np.cos(fine * angle)
        right[:, 2 * fine - 1] = np.sin(fine * angle)
    return left.reshape(2 * COARSE, DEPTH).astype(np.float32), right.astype(np.float32)


def per_device(spectra, bad_channels, tile_list):
    rows = spectra.reshape(F * 4, SHARD)
    return fused(rows, bad_channels.reshape(1, SHARD), tile_list.T)


def solution(mesh):
    placed = (P(None, "tm", None, "chan"), P("chan"), P("chan", None))
    return jax.shard_map(
        per_device,
        mesh=mesh,
        in_specs=placed,
        out_specs=P(("chan", "tm"), None, None, None),
        check_vma=False,
    )
```

```python
import math

import jax
import jax.numpy as jnp
import numpy as np
from jax import lax
from jax.experimental import pallas as pl
from jax.experimental.pallas import tpu as pltpu
from jax.sharding import PartitionSpec as P

F = 64
HOURS = 8
LAGS = 32
TILE = 128
EPSILON = 1e-06

PLANE = 32
SHARD = 96
HALF = 24
ROWS = 8
DEPTH = PLANE * ROWS
SLOTS = 4
FINE = 4
COARSE = LAGS // FINE
FAR = 20
NEAR = (0, 2, 6, 8, 24)
CROSS = tuple((near + dc, dc) for near in NEAR for dc in range(2))
INSIDE = tuple(j for j in range(PLANE) if (j & ~1) ^ FAR not in NEAR)
PIECE = ROWS // 2
ROUNDS = (((0, 0), (0, 1)), ((1, 0), (2, 0)), ((1, 1), (2, 1)), ((3, 0), (3, 1)))
MESH_ID = pl.DeviceIdType.MESH


def load_blocks(got, i, bins, left_table, cosines, sines, swap, eye, lhs, rhs):
    starts = [pl.multiple_of(TILE * f, TILE) for f in bins]

    def block(side):
        halves = [got[:, h, 2 * i + side].astype(jnp.float32).reshape(TILE, TILE) for h in range(2)]
        return jnp.concatenate(halves, axis=0)

    a = lax.dot_general(
        eye[...], block(0).astype(jnp.bfloat16), (((1,), (1,)), ((), ())), preferred_element_type=jnp.float32
    )
    turned = jnp.dot(a.astype(jnp.bfloat16), swap[...], preferred_element_type=jnp.float32)
    for h, start in enumerate(starts):
        cols = slice(h * TILE, (h + 1) * TILE)
        for c in range(COARSE):
            cos = left_table[2 * c : 2 * c + 1, pl.ds(start, TILE)]
            sin = left_table[2 * c + 1 : 2 * c + 2, pl.ds(start, TILE)]
            lhs[pl.ds(c * TILE, TILE), cols] = (a[:, cols] * cos + turned[:, cols] * sin).astype(jnp.bfloat16)
    b = block(1)
    exact = b.astype(jnp.bfloat16)
    turned = jnp.dot(swap[...], exact, preferred_element_type=jnp.float32)
    rhs[:, 0:TILE] = exact
    for h, start in enumerate(starts):
        rows = slice(h * TILE, (h + 1) * TILE)
        for fine in range(1, FINE):
            cos = cosines[fine - 1, pl.ds(start, TILE)]
            sin = sines[fine - 1, pl.ds(start, TILE)]
            rhs[rows, fine * TILE : (fine + 1) * TILE] = (b[rows] * cos + turned[rows] * sin).astype(jnp.bfloat16)


def lag_products(lhs, rhs, c, add):
    for n in range(2):
        weights = rhs[:, 2 * n * TILE : (2 * n + 2) * TILE]
        res = jnp.dot(lhs[c * TILE : (c + 2) * TILE, :], weights, preferred_element_type=jnp.float32)
        for dc in range(2):
            for dn in range(2):
                lag = FINE * (c + dc) + 2 * n + dn
                add(lag, res[dc * TILE : (dc + 1) * TILE, dn * TILE : (dn + 1) * TILE])


def finish_kernel(last, partial, left_table, cosines, sines, swap, eye, out_hbm, stage, lhs, rhs, sems):
    copies = []
    for i in range(2):
        load_blocks(last, i, (0, 1), left_table, cosines, sines, swap, eye, lhs.at[i], rhs.at[i])
        for c in range(0, COARSE, 2):
            def put(lag, value):
                stage[i, lag] = partial[i, lag] + value

            lag_products(lhs.at[i], rhs.at[i], c, put)
            lags = pl.ds(FINE * c, 2 * FINE)
            copies.append(pltpu.make_async_copy(stage.at[i, lags], out_hbm.at[i, lags], sems.at[len(copies)]))
            copies[-1].start()
    for copy in copies:
        copy.wait()


def fused_kernel(
    spec_hbm, bad_hbm, tile_hbm, left_hbm, right_hbm, out_ref, last, left_table, cosines, sines, swap, eye,
    spec, bad_ref, tile_ref, right_table, white, mine, mine_other, tiles_in, tiles, zb00, zb01, zb10, zb11, zb20, zb21, zb30, zb31, pack, got, lhs, rhs, other0, other1,
    sem_in, sem_a_send, sem_a_recv, sem_b_recv, sem_t_send, sem_t_recv, sem_t_local, sem_z_send, sem_z_recv,
    sem_p_send, sem_p_recv,
):
    zbs = ((zb00, zb01), (zb10, zb11), (zb20, zb21), (zb30, zb31))
    chan, tm = lax.axis_index("chan"), lax.axis_index("tm")
    half = lax.shift_right_logical(chan, 5)
    me = lax.bitwise_and(chan, PLANE - 1)
    z = half * 4 + tm
    odd = lax.bitwise_and(z, 1)

    loads = [
        pltpu.make_async_copy(src, dst, sem_in.at[i])
        for i, (src, dst) in enumerate(
            ((spec_hbm, spec), (bad_hbm, bad_ref), (tile_hbm, tile_ref), (left_hbm, left_table), (right_hbm, right_table))
        )
    ]
    for load in loads:
        load.start()

    def plane_peer(j):
        k = lax.bitwise_xor(me, j)
        return k, (lax.bitwise_xor(chan, j), tm)

    def each_peer(act):
        def four(i, carry):
            for u in range(4):
                act(lax.bitwise_xor(4 * i + u, FAR))
            return carry

        lax.fori_loop(0, FAR // 4, four, 0)
        for u in range(FAR + 1, FAR + 4):
            act(u ^ FAR)
        lax.fori_loop(FAR // 4 + 1, PLANE // 4, four, 0)

    def plane(step):
        return lax.bitwise_and(z + step, 7)

    def z_peer(step, j=0):
        zz = plane(step)
        return lax.shift_right_logical(zz, 2) * PLANE + lax.bitwise_xor(me, j), lax.bitwise_and(zz, 3)

    def base(step):
        return lax.shift_right_logical(plane(step), 2) * HALF

    barrier = pltpu.get_barrier_semaphore()

    def greet(j):
        _, dev = plane_peer(j)
        pl.semaphore_signal(barrier, inc=1, device_id=dev, device_id_type=MESH_ID)

    each_peer(greet)
    for step, j in [(3, 0), (5, 0), (2, 0), (6, 0)] + [(step, j) for j, _ in CROSS for step in (1, 7)]:
        pl.semaphore_signal(barrier, inc=1, device_id=z_peer(step, j), device_id_type=MESH_ID)

    for load in loads[:2]:
        load.wait()
    values = spec[...].astype(jnp.float32).reshape(F // 2, ROWS, SHARD)
    squares = jnp.sum(values * values, axis=0)
    row = lax.broadcasted_iota(jnp.int32, (ROWS, SHARD), 0)
    first = (row % 4) < 2
    power0 = jnp.sum(jnp.where(first, squares, 0.0), axis=0, keepdims=True) / (2 * F)
    power1 = jnp.sum(jnp.where(first, 0.0, squares), axis=0, keepdims=True) / (2 * F)
    scale = lax.rsqrt(jnp.where(first, power0, power1) + EPSILON)
    keep = (1 - bad_ref[...]).astype(jnp.float32)
    whitened = values * scale[None] * keep[None]
    padded = jnp.concatenate([whitened, jnp.zeros((F // 2, ROWS, TILE - SHARD), jnp.float32)], axis=2)
    padded = padded.astype(jnp.bfloat16)
    white[...] = padded

    pl.semaphore_wait(barrier, PLANE - 1 + 4 + 2 * len(CROSS))

    for kind, dst, sem in ((odd, mine, sem_a_recv), (1 - odd, mine_other, sem_b_recv)):
        shift = kind * FAR
        pltpu.make_async_copy(white.at[lax.bitwise_xor(me, shift)], dst.at[me], sem).start()

        def spread(j):
            k, dev = plane_peer(j)
            pltpu.make_async_remote_copy(
                src_ref=white.at[lax.bitwise_xor(k, shift)], dst_ref=dst.at[me], send_sem=sem_a_send, recv_sem=sem,
                device_id=dev, device_id_type=MESH_ID,
            ).start()

        each_peer(spread)

    for load in loads[2:]:
        load.wait()
    pltpu.make_async_copy(tile_ref, tiles_in.at[0], sem_t_recv).start()

    def send_tiles(slot, dev):
        pltpu.make_async_remote_copy(
            src_ref=tile_ref, dst_ref=tiles_in.at[slot], send_sem=sem_t_send, recv_sem=sem_t_recv,
            device_id=dev, device_id_type=MESH_ID,
        ).start()

    for n, j in enumerate(INSIDE[1:], 1):
        send_tiles(n, plane_peer(j)[1])
    for n, (j, dc) in enumerate(CROSS, len(INSIDE)):
        send_tiles(n, z_peer((1, 7)[dc], j))

    out_ref[...] = jnp.zeros_like(out_ref)
    row = lax.broadcasted_iota(jnp.int32, (DEPTH, DEPTH), 0)
    ahead = lax.broadcasted_iota(jnp.int32, (DEPTH, DEPTH), 1) - row
    even = lax.bitwise_and(row, 1) == 0
    to_re = jnp.where(even, jnp.where(ahead == 1, 1.0, 0.0), jnp.where(ahead == -1, -1.0, 0.0))
    swap[...] = to_re.astype(jnp.bfloat16)
    eye[...] = jnp.where(ahead[:TILE, :TILE] == 0, 1.0, 0.0).astype(jnp.bfloat16)
    for fine in range(1, FINE):
        column = 2 * (fine - 1)
        cosines[fine - 1] = jnp.broadcast_to(right_table[:, column : column + 1], (DEPTH, TILE))
        sines[fine - 1] = jnp.broadcast_to(right_table[:, column + 1 : column + 2], (DEPTH, TILE))

    lane = lax.broadcasted_iota(jnp.int32, (ROWS, TILE), 1)
    own = half * HALF

    def to_blocks(src, dst, start):
        for g in range(PLANE // 4):
            s0, s1, s2, s3 = (src[4 * g + i].astype(jnp.float32) for i in range(4))
            s1 = pltpu.roll(s1, 96, 1)
            s2 = pltpu.roll(s2, 64, 1)
            s3 = pltpu.roll(s3, 32, 1)
            for n, merged in enumerate(
                (jnp.where(lane < 96, s0, s1), jnp.where(lane < 64, s1, s2), jnp.where(lane < 32, s2, s3))
            ):
                for f in range(2):
                    dst[f][start + 3 * g + n] = merged[f * PIECE : (f + 1) * PIECE].astype(jnp.bfloat16)

    def send_z(src, chunk, f, at, count, step):
        pltpu.make_async_remote_copy(
            src_ref=src, dst_ref=zbs[chunk][f].at[pl.ds(at, count)],
            send_sem=sem_z_send, recv_sem=sem_z_recv.at[chunk, f],
            device_id=z_peer(step), device_id_type=MESH_ID,
        ).start()

    pltpu.make_async_copy(mine, mine, sem_a_recv).wait()
    to_blocks(mine, zbs[3], own)
    for f in range(2):
        for step in (2, 6):
            send_z(zbs[3][f].at[pl.ds(own, HALF)], 0, f, own, HALF, step)
    pltpu.make_async_copy(mine_other, mine_other, sem_b_recv).wait()
    to_blocks(mine_other, (other0, other1), 0)
    for f, other in enumerate((other0, other1)):
        for step, chunk in ((7, 1), (3, 1), (1, 2), (5, 2)):
            send_z(other, chunk, f, own, HALF, step)

    pltpu.make_async_copy(tiles_in, tiles_in, sem_t_recv).wait()
    to_smem = pltpu.make_async_copy(tiles_in, tiles, sem_t_local)
    to_smem.start()
    to_smem.wait()

    slot = lax.bitwise_xor(me, odd * FAR)
    wanted = [(plane_peer(j)[1], tm) for j in INSIDE]
    for j, dc in CROSS:
        dev = z_peer((7, 1)[dc], j)
        wanted.append((dev, dev[1]))

    def landing(n):
        return got.at[n, slot] if n < 3 else last.at[slot]

    def deliver(src, dst, n, to):
        pltpu.make_async_remote_copy(
            src_ref=src, dst_ref=dst, send_sem=sem_p_send, recv_sem=sem_p_recv.at[n],
            device_id=wanted[to][0], device_id_type=MESH_ID,
        ).start()

    for n, pieces in enumerate(ROUNDS):
        whole = pieces[0][0] == pieces[1][0]
        for h, (chunk, f) in enumerate(pieces):
            zb = zbs[chunk][f]
            late = zb if chunk < 3 else zb.at[pl.ds(base(4), HALF)]
            pltpu.make_async_copy(late, late, sem_z_recv.at[chunk, f]).wait()
            if chunk == 0:
                for step, at in ((2, base(6)), (6, base(2) + HALF // 2)):
                    send_z(zb.at[pl.ds(at, HALF // 2)], 3, f, at, HALF // 2, step)
            for to in range(0, PLANE, 4):
                places = [(to + u, s) for u in range(4) for s in range(SLOTS)]
                blocks = [zb[tiles[i, s % 2, 2 * wanted[i][1] + s // 2]] for i, s in places]
                for (i, s), block in zip(places, blocks):
                    pack[n, i, h, s] = block
            if n == 1 and h == 0:
                for to in range(len(INSIDE), PLANE):
                    deliver(pack.at[0, to], landing(0), 0, to)
            if not whole:
                for to in reversed(range(1, PLANE)):
                    deliver(pack.at[n, to, h], landing(n).at[h], n, to)
        pltpu.make_async_copy(pack.at[n, 0], landing(n), sem_p_recv.at[n]).start()
        if whole:
            for to in reversed(range(1, len(INSIDE) if n == 0 else PLANE)):
                deliver(pack.at[n, to], landing(n), n, to)

    def correlate(chunk, carry):
        part = got.at[chunk]
        pltpu.make_async_copy(part, part, sem_p_recv.at[chunk]).wait()

        def one_tile(i, carry):
            def add(lag, value):
                out_ref[i, lag] += value

            bins = (lax.shift_right_logical(chunk, 1), 1 - lax.bitwise_and(chunk, 1))
            load_blocks(part, i, bins, left_table, cosines, sines, swap, eye, lhs, rhs)
            for c in range(0, COARSE, 2):
                lag_products(lhs, rhs, c, add)
            return carry

        return lax.fori_loop(0, 2, one_tile, carry)

    lax.fori_loop(0, 3, correlate, 0)

    pltpu.make_async_copy(last, last, sem_p_recv.at[3]).wait()
    sent = white.at[pl.ds(0, PLANE - 1)]
    for _ in range(2):
        pltpu.make_async_copy(sent, sent, sem_a_send).wait()
    sent = tiles_in.at[pl.ds(0, PLANE - 1)]
    pltpu.make_async_copy(sent, sent, sem_t_send).wait()
    for _ in range(7):
        for f in range(2):
            sent = zbs[3][f].at[pl.ds(0, HALF)]
            pltpu.make_async_copy(sent, sent, sem_z_send).wait()
    sent = pack.at[:, pl.ds(0, PLANE - 1)]
    pltpu.make_async_copy(sent, sent, sem_p_send).wait()


def fused(spectra, bad, tile_pairs):
    vmem = pl.BlockSpec(memory_space=pltpu.VMEM)
    slab = pltpu.VMEM((2 * HALF, PIECE, TILE), jnp.bfloat16)
    dma = pltpu.SemaphoreType.DMA
    left_table, right_table = lag_tables()
    block = (PLANE, 2, SLOTS, PIECE, TILE)
    table = (FINE - 1, DEPTH, TILE)
    partial, *rest = pl.pallas_call(
        fused_kernel,
        out_shape=[
            jax.ShapeDtypeStruct((2, LAGS, TILE, TILE), jnp.float32),
            jax.ShapeDtypeStruct(block, jnp.bfloat16),
            jax.ShapeDtypeStruct((2 * COARSE, DEPTH), jnp.float32),
            jax.ShapeDtypeStruct(table, jnp.float32),
            jax.ShapeDtypeStruct(table, jnp.float32),
            jax.ShapeDtypeStruct((DEPTH, DEPTH), jnp.bfloat16),
            jax.ShapeDtypeStruct((TILE, TILE), jnp.bfloat16),
        ],
        in_specs=[pl.BlockSpec(memory_space=pltpu.HBM)] * 5,
        out_specs=[vmem] * 7,
        scratch_shapes=[
            pltpu.VMEM((F * 4, SHARD), jnp.bfloat16),
            pltpu.VMEM((1, SHARD), jnp.int32),
            pltpu.VMEM((2, 8), jnp.int32),
            pltpu.VMEM((DEPTH, TILE), jnp.float32),
            pltpu.VMEM((PLANE, ROWS, TILE), jnp.bfloat16),
            pltpu.VMEM((PLANE, ROWS, TILE), jnp.bfloat16),
            pltpu.VMEM((PLANE, ROWS, TILE), jnp.bfloat16),
            pltpu.VMEM((PLANE, 2, 8), jnp.int32),
            pltpu.SMEM((PLANE, 2, 8), jnp.int32),
            slab, slab, slab, slab, slab, slab, slab, slab,
            pltpu.VMEM((4, *block), jnp.bfloat16),
            pltpu.VMEM((3, *block), jnp.bfloat16),
            pltpu.VMEM((COARSE * TILE, DEPTH), jnp.bfloat16),
            pltpu.VMEM((DEPTH, FINE * TILE), jnp.bfloat16),
            pltpu.VMEM((HALF, PIECE, TILE), jnp.bfloat16),
            pltpu.VMEM((HALF, PIECE, TILE), jnp.bfloat16),
            dma((5,)), dma, dma, dma, dma, dma, dma, dma, dma((4, 2)), dma, dma((4,)),
        ],
        compiler_params=pltpu.CompilerParams(
            collective_id=0, has_side_effects=True, vmem_limit_bytes=16 << 20
        ),
        name="fused",
    )(*(
        pltpu.with_memory_space_constraint(v, pltpu.HBM)
        for v in (spectra, bad, tile_pairs, jnp.asarray(left_table), jnp.asarray(right_table))
    ))
    return pl.pallas_call(
        finish_kernel,
        out_shape=jax.ShapeDtypeStruct((2, LAGS, TILE, TILE), jnp.float32),
        in_specs=[vmem] * 7,
        out_specs=pl.BlockSpec(memory_space=pltpu.HBM),
        scratch_shapes=[
            pltpu.VMEM((2, LAGS, TILE, TILE), jnp.float32),
            pltpu.VMEM((2, COARSE * TILE, DEPTH), jnp.bfloat16),
            pltpu.VMEM((2, DEPTH, FINE * TILE), jnp.bfloat16),
            dma((COARSE,)),
        ],
        compiler_params=pltpu.CompilerParams(vmem_limit_bytes=12 << 20),
        name="finish",
    )(rest[0], partial, *rest[1:])


def lag_tables():
    row = np.arange(DEPTH)
    bin_number = 2 * (row % TILE // PIECE) + row // TILE + 1.0
    angle = np.pi / F * bin_number
    coarse = FINE * np.arange(COARSE) - LAGS // 2
    norm = 1.0 / math.sqrt(F * HOURS)
    left = np.stack([np.cos(coarse[:, None] * angle), np.sin(coarse[:, None] * angle)], axis=1) * norm
    right = np.zeros((DEPTH, TILE))
    for fine in range(1, FINE):
        right[:, 2 * fine - 2] = np.cos(fine * angle)
        right[:, 2 * fine - 1] = np.sin(fine * angle)
    return left.reshape(2 * COARSE, DEPTH).astype(np.float32), right.astype(np.float32)


def per_device(spectra, bad_channels, tile_list):
    rows = spectra.reshape(F * 4, SHARD)
    return fused(rows, bad_channels.reshape(1, SHARD), tile_list.T)


def solution(mesh):
    placed = (P(None, "tm", None, "chan"), P("chan"), P("chan", None))
    return jax.shard_map(
        per_device,
        mesh=mesh,
        in_specs=placed,
        out_specs=P(("chan", "tm"), None, None, None),
        check_vma=False,
    )
```

```python
import math

import jax
import jax.numpy as jnp
import numpy as np
from jax import lax
from jax.experimental import pallas as pl
from jax.experimental.pallas import tpu as pltpu
from jax.sharding import PartitionSpec as P

F = 64
HOURS = 8
LAGS = 32
TILE = 128
EPSILON = 1e-06

PLANE = 32
SHARD = 96
HALF = 24
ROWS = 8
DEPTH = PLANE * ROWS
SLOTS = 4
FINE = 4
COARSE = LAGS // FINE
FAR = 20
NEAR = (0, 2, 6, 8, 24)
CROSS = tuple((near + dc, dc) for near in NEAR for dc in range(2))
INSIDE = tuple(j for j in range(PLANE) if (j & ~1) ^ FAR not in NEAR)
PIECE = ROWS // 2
ROUNDS = (((0, 0), (0, 1)), ((1, 0), (2, 0)), ((1, 1), (2, 1)), ((3, 0), (3, 1)))
MESH_ID = pl.DeviceIdType.MESH


def load_blocks(got, i, bins, left_table, cosines, sines, swap, eye, lhs, rhs):
    starts = [pl.multiple_of(TILE * f, TILE) for f in bins]

    def block(side):
        halves = [got[:, h, 2 * i + side].astype(jnp.float32).reshape(TILE, TILE) for h in range(2)]
        return jnp.concatenate(halves, axis=0)

    a = lax.dot_general(
        eye[...], block(0).astype(jnp.bfloat16), (((1,), (1,)), ((), ())), preferred_element_type=jnp.float32
    )
    turned = jnp.dot(a.astype(jnp.bfloat16), swap[...], preferred_element_type=jnp.float32)
    for h, start in enumerate(starts):
        cols = slice(h * TILE, (h + 1) * TILE)
        for c in range(COARSE):
            cos = left_table[2 * c : 2 * c + 1, pl.ds(start, TILE)]
            sin = left_table[2 * c + 1 : 2 * c + 2, pl.ds(start, TILE)]
            lhs[pl.ds(c * TILE, TILE), cols] = (a[:, cols] * cos + turned[:, cols] * sin).astype(jnp.bfloat16)
    b = block(1)
    exact = b.astype(jnp.bfloat16)
    turned = jnp.dot(swap[...], exact, preferred_element_type=jnp.float32)
    rhs[:, 0:TILE] = exact
    for h, start in enumerate(starts):
        rows = slice(h * TILE, (h + 1) * TILE)
        for fine in range(1, FINE):
            cos = cosines[fine - 1, pl.ds(start, TILE)]
            sin = sines[fine - 1, pl.ds(start, TILE)]
            rhs[rows, fine * TILE : (fine + 1) * TILE] = (b[rows] * cos + turned[rows] * sin).astype(jnp.bfloat16)


def lag_products(lhs, rhs, c, add):
    for n in range(2):
        weights = jnp.concatenate([part[:, 2 * n * TILE : (2 * n + 2) * TILE] for part in rhs], axis=0)
        rotated = jnp.concatenate([part[c * TILE : (c + 2) * TILE, :] for part in lhs], axis=1)
        res = jnp.dot(rotated, weights, preferred_element_type=jnp.float32)
        for dc in range(2):
            for dn in range(2):
                lag = FINE * (c + dc) + 2 * n + dn
                add(lag, res[dc * TILE : (dc + 1) * TILE, dn * TILE : (dn + 1) * TILE])


def finish_kernel(last, lhs_late, rhs_late, partial, left_table, cosines, sines, swap, eye, out_hbm, stage, lhs, rhs, sems):
    copies = []
    for i in range(2):
        load_blocks(last, i, (0, 1), left_table, cosines, sines, swap, eye, lhs.at[i], rhs.at[i])
        for c in range(0, COARSE, 2):
            def put(lag, value):
                stage[i, lag] = partial[i, lag] + value

            lag_products((lhs_late.at[i], lhs.at[i]), (rhs_late.at[i], rhs.at[i]), c, put)
            lags = pl.ds(FINE * c, 2 * FINE)
            copies.append(pltpu.make_async_copy(stage.at[i, lags], out_hbm.at[i, lags], sems.at[len(copies)]))
            copies[-1].start()
    for copy in copies:
        copy.wait()


def fused_kernel(
    spec_hbm, bad_hbm, tile_hbm, left_hbm, right_hbm, out_ref, last, lhs_late, rhs_late, left_table, cosines, sines, swap, eye,
    spec, bad_ref, tile_ref, right_table, white, mine, mine_other, tiles_in, tiles, zb00, zb01, zb10, zb11, zb20, zb21, zb30, zb31, pack, got, lhs, rhs, other0, other1,
    sem_in, sem_a_send, sem_a_recv, sem_b_recv, sem_t_send, sem_t_recv, sem_t_local, sem_z_send, sem_z_recv,
    sem_p_send, sem_p_recv,
):
    zbs = ((zb00, zb01), (zb10, zb11), (zb20, zb21), (zb30, zb31))
    chan, tm = lax.axis_index("chan"), lax.axis_index("tm")
    half = lax.shift_right_logical(chan, 5)
    me = lax.bitwise_and(chan, PLANE - 1)
    z = half * 4 + tm
    odd = lax.bitwise_and(z, 1)

    loads = [
        pltpu.make_async_copy(src, dst, sem_in.at[i])
        for i, (src, dst) in enumerate(
            ((spec_hbm, spec), (bad_hbm, bad_ref), (tile_hbm, tile_ref), (left_hbm, left_table), (right_hbm, right_table))
        )
    ]
    for load in loads:
        load.start()

    def plane_peer(j):
        k = lax.bitwise_xor(me, j)
        return k, (lax.bitwise_xor(chan, j), tm)

    def each_peer(act):
        def four(i, carry):
            for u in range(4):
                act(lax.bitwise_xor(4 * i + u, FAR))
            return carry

        lax.fori_loop(0, FAR // 4, four, 0)
        for u in range(FAR + 1, FAR + 4):
            act(u ^ FAR)
        lax.fori_loop(FAR // 4 + 1, PLANE // 4, four, 0)

    def plane(step):
        return lax.bitwise_and(z + step, 7)

    def z_peer(step, j=0):
        zz = plane(step)
        return lax.shift_right_logical(zz, 2) * PLANE + lax.bitwise_xor(me, j), lax.bitwise_and(zz, 3)

    def base(step):
        return lax.shift_right_logical(plane(step), 2) * HALF

    barrier = pltpu.get_barrier_semaphore()

    def greet(j):
        _, dev = plane_peer(j)
        pl.semaphore_signal(barrier, inc=1, device_id=dev, device_id_type=MESH_ID)

    each_peer(greet)
    for step, j in [(3, 0), (5, 0), (2, 0), (6, 0)] + [(step, j) for j, _ in CROSS for step in (1, 7)]:
        pl.semaphore_signal(barrier, inc=1, device_id=z_peer(step, j), device_id_type=MESH_ID)

    for load in loads[:2]:
        load.wait()
    values = spec[...].astype(jnp.float32).reshape(F // 2, ROWS, SHARD)
    squares = jnp.sum(values * values, axis=0)
    row = lax.broadcasted_iota(jnp.int32, (ROWS, SHARD), 0)
    first = (row % 4) < 2
    power0 = jnp.sum(jnp.where(first, squares, 0.0), axis=0, keepdims=True) / (2 * F)
    power1 = jnp.sum(jnp.where(first, 0.0, squares), axis=0, keepdims=True) / (2 * F)
    scale = lax.rsqrt(jnp.where(first, power0, power1) + EPSILON)
    keep = (1 - bad_ref[...]).astype(jnp.float32)
    whitened = values * scale[None] * keep[None]
    padded = jnp.concatenate([whitened, jnp.zeros((F // 2, ROWS, TILE - SHARD), jnp.float32)], axis=2)
    padded = padded.astype(jnp.bfloat16)
    white[...] = padded

    pl.semaphore_wait(barrier, PLANE - 1 + 4 + 2 * len(CROSS))

    for kind, dst, sem in ((odd, mine, sem_a_recv), (1 - odd, mine_other, sem_b_recv)):
        shift = kind * FAR
        pltpu.make_async_copy(white.at[lax.bitwise_xor(me, shift)], dst.at[me], sem).start()

        def spread(j):
            k, dev = plane_peer(j)
            pltpu.make_async_remote_copy(
                src_ref=white.at[lax.bitwise_xor(k, shift)], dst_ref=dst.at[me], send_sem=sem_a_send, recv_sem=sem,
                device_id=dev, device_id_type=MESH_ID,
            ).start()

        each_peer(spread)

    for load in loads[2:]:
        load.wait()
    pltpu.make_async_copy(tile_ref, tiles_in.at[0], sem_t_recv).start()

    def send_tiles(slot, dev):
        pltpu.make_async_remote_copy(
            src_ref=tile_ref, dst_ref=tiles_in.at[slot], send_sem=sem_t_send, recv_sem=sem_t_recv,
            device_id=dev, device_id_type=MESH_ID,
        ).start()

    for n, j in enumerate(INSIDE[1:], 1):
        send_tiles(n, plane_peer(j)[1])
    for n, (j, dc) in enumerate(CROSS, len(INSIDE)):
        send_tiles(n, z_peer((1, 7)[dc], j))

    out_ref[...] = jnp.zeros_like(out_ref)
    row = lax.broadcasted_iota(jnp.int32, (DEPTH, DEPTH), 0)
    ahead = lax.broadcasted_iota(jnp.int32, (DEPTH, DEPTH), 1) - row
    even = lax.bitwise_and(row, 1) == 0
    to_re = jnp.where(even, jnp.where(ahead == 1, 1.0, 0.0), jnp.where(ahead == -1, -1.0, 0.0))
    swap[...] = to_re.astype(jnp.bfloat16)
    eye[...] = jnp.where(ahead[:TILE, :TILE] == 0, 1.0, 0.0).astype(jnp.bfloat16)
    for fine in range(1, FINE):
        column = 2 * (fine - 1)
        cosines[fine - 1] = jnp.broadcast_to(right_table[:, column : column + 1], (DEPTH, TILE))
        sines[fine - 1] = jnp.broadcast_to(right_table[:, column + 1 : column + 2], (DEPTH, TILE))

    lane = lax.broadcasted_iota(jnp.int32, (ROWS, TILE), 1)
    own = half * HALF

    def to_blocks(src, dst, start):
        for g in range(PLANE // 4):
            s0, s1, s2, s3 = (src[4 * g + i].astype(jnp.float32) for i in range(4))
            s1 = pltpu.roll(s1, 96, 1)
            s2 = pltpu.roll(s2, 64, 1)
            s3 = pltpu.roll(s3, 32, 1)
            for n, merged in enumerate(
                (jnp.where(lane < 96, s0, s1), jnp.where(lane < 64, s1, s2), jnp.where(lane < 32, s2, s3))
            ):
                for f in range(2):
                    dst[f][start + 3 * g + n] = merged[f * PIECE : (f + 1) * PIECE].astype(jnp.bfloat16)

    def send_z(src, chunk, f, at, count, step):
        pltpu.make_async_remote_copy(
            src_ref=src, dst_ref=zbs[chunk][f].at[pl.ds(at, count)],
            send_sem=sem_z_send, recv_sem=sem_z_recv.at[chunk, f],
            device_id=z_peer(step), device_id_type=MESH_ID,
        ).start()

    pltpu.make_async_copy(mine, mine, sem_a_recv).wait()
    to_blocks(mine, zbs[3], own)
    for f in range(2):
        for step in (2, 6):
            send_z(zbs[3][f].at[pl.ds(own, HALF)], 0, f, own, HALF, step)
    pltpu.make_async_copy(mine_other, mine_other, sem_b_recv).wait()
    to_blocks(mine_other, (other0, other1), 0)
    for f, other in enumerate((other0, other1)):
        for step, chunk in ((7, 1), (3, 1), (1, 2), (5, 2)):
            send_z(other, chunk, f, own, HALF, step)

    pltpu.make_async_copy(tiles_in, tiles_in, sem_t_recv).wait()
    to_smem = pltpu.make_async_copy(tiles_in, tiles, sem_t_local)
    to_smem.start()
    to_smem.wait()

    slot = lax.bitwise_xor(me, odd * FAR)
    wanted = [(plane_peer(j)[1], tm) for j in INSIDE]
    for j, dc in CROSS:
        dev = z_peer((7, 1)[dc], j)
        wanted.append((dev, dev[1]))

    def landing(n):
        return got.at[n, slot] if n < 3 else last.at[slot]

    def deliver(src, dst, n, to):
        pltpu.make_async_remote_copy(
            src_ref=src, dst_ref=dst, send_sem=sem_p_send, recv_sem=sem_p_recv.at[n],
            device_id=wanted[to][0], device_id_type=MESH_ID,
        ).start()

    for n, pieces in enumerate(ROUNDS):
        whole = pieces[0][0] == pieces[1][0]
        for h, (chunk, f) in enumerate(pieces):
            zb = zbs[chunk][f]
            late = zb if chunk < 3 else zb.at[pl.ds(base(4), HALF)]
            pltpu.make_async_copy(late, late, sem_z_recv.at[chunk, f]).wait()
            if chunk == 0:
                for step, at in ((2, base(6)), (6, base(2) + HALF // 2)):
                    send_z(zb.at[pl.ds(at, HALF // 2)], 3, f, at, HALF // 2, step)
            for to in range(0, PLANE, 4):
                places = [(to + u, s) for u in range(4) for s in range(SLOTS)]
                blocks = [zb[tiles[i, s % 2, 2 * wanted[i][1] + s // 2]] for i, s in places]
                for (i, s), block in zip(places, blocks):
                    pack[n, i, h, s] = block
            if n == 1 and h == 0:
                for to in range(len(INSIDE), PLANE):
                    deliver(pack.at[0, to], landing(0), 0, to)
            if not whole:
                for to in reversed(range(1, PLANE)):
                    deliver(pack.at[n, to, h], landing(n).at[h], n, to)
        pltpu.make_async_copy(pack.at[n, 0], landing(n), sem_p_recv.at[n]).start()
        if whole:
            for to in reversed(range(1, len(INSIDE) if n == 0 else PLANE)):
                deliver(pack.at[n, to], landing(n), n, to)

    def correlate(chunk, carry):
        part = got.at[chunk]
        pltpu.make_async_copy(part, part, sem_p_recv.at[chunk]).wait()

        def one_tile(i, carry):
            def add(lag, value):
                out_ref[i, lag] += value

            bins = (0, 1 - chunk)
            load_blocks(part, i, bins, left_table, cosines, sines, swap, eye, lhs, rhs)
            for c in range(0, COARSE, 2):
                lag_products((lhs,), (rhs,), c, add)
            return carry

        return lax.fori_loop(0, 2, one_tile, carry)

    lax.fori_loop(0, 2, correlate, 0)

    pltpu.make_async_copy(got.at[2], got.at[2], sem_p_recv.at[2]).wait()

    def make_ready(i, carry):
        load_blocks(
            got.at[2], i, (1, 1), left_table, cosines, sines, swap, eye, lhs_late.at[i], rhs_late.at[i]
        )
        return carry

    lax.fori_loop(0, 2, make_ready, 0)

    pltpu.make_async_copy(last, last, sem_p_recv.at[3]).wait()
    sent = white.at[pl.ds(0, PLANE - 1)]
    for _ in range(2):
        pltpu.make_async_copy(sent, sent, sem_a_send).wait()
    sent = tiles_in.at[pl.ds(0, PLANE - 1)]
    pltpu.make_async_copy(sent, sent, sem_t_send).wait()
    for _ in range(7):
        for f in range(2):
            sent = zbs[3][f].at[pl.ds(0, HALF)]
            pltpu.make_async_copy(sent, sent, sem_z_send).wait()
    sent = pack.at[:, pl.ds(0, PLANE - 1)]
    pltpu.make_async_copy(sent, sent, sem_p_send).wait()


def fused(spectra, bad, tile_pairs):
    vmem = pl.BlockSpec(memory_space=pltpu.VMEM)
    slab = pltpu.VMEM((2 * HALF, PIECE, TILE), jnp.bfloat16)
    dma = pltpu.SemaphoreType.DMA
    left_table, right_table = lag_tables()
    block = (PLANE, 2, SLOTS, PIECE, TILE)
    table = (FINE - 1, DEPTH, TILE)
    partial, *rest = pl.pallas_call(
        fused_kernel,
        out_shape=[
            jax.ShapeDtypeStruct((2, LAGS, TILE, TILE), jnp.float32),
            jax.ShapeDtypeStruct(block, jnp.bfloat16),
            jax.ShapeDtypeStruct((2, COARSE * TILE, DEPTH), jnp.bfloat16),
            jax.ShapeDtypeStruct((2, DEPTH, FINE * TILE), jnp.bfloat16),
            jax.ShapeDtypeStruct((2 * COARSE, DEPTH), jnp.float32),
            jax.ShapeDtypeStruct(table, jnp.float32),
            jax.ShapeDtypeStruct(table, jnp.float32),
            jax.ShapeDtypeStruct((DEPTH, DEPTH), jnp.bfloat16),
            jax.ShapeDtypeStruct((TILE, TILE), jnp.bfloat16),
        ],
        in_specs=[pl.BlockSpec(memory_space=pltpu.HBM)] * 5,
        out_specs=[vmem] * 9,
        scratch_shapes=[
            pltpu.VMEM((F * 4, SHARD), jnp.bfloat16),
            pltpu.VMEM((1, SHARD), jnp.int32),
            pltpu.VMEM((2, 8), jnp.int32),
            pltpu.VMEM((DEPTH, TILE), jnp.float32),
            pltpu.VMEM((PLANE, ROWS, TILE), jnp.bfloat16),
            pltpu.VMEM((PLANE, ROWS, TILE), jnp.bfloat16),
            pltpu.VMEM((PLANE, ROWS, TILE), jnp.bfloat16),
            pltpu.VMEM((PLANE, 2, 8), jnp.int32),
            pltpu.SMEM((PLANE, 2, 8), jnp.int32),
            slab, slab, slab, slab, slab, slab, slab, slab,
            pltpu.VMEM((4, *block), jnp.bfloat16),
            pltpu.VMEM((3, *block), jnp.bfloat16),
            pltpu.VMEM((COARSE * TILE, DEPTH), jnp.bfloat16),
            pltpu.VMEM((DEPTH, FINE * TILE), jnp.bfloat16),
            pltpu.VMEM((HALF, PIECE, TILE), jnp.bfloat16),
            pltpu.VMEM((HALF, PIECE, TILE), jnp.bfloat16),
            dma((5,)), dma, dma, dma, dma, dma, dma, dma, dma((4, 2)), dma, dma((4,)),
        ],
        compiler_params=pltpu.CompilerParams(
            collective_id=0, has_side_effects=True, vmem_limit_bytes=16 << 20
        ),
        name="fused",
    )(*(
        pltpu.with_memory_space_constraint(v, pltpu.HBM)
        for v in (spectra, bad, tile_pairs, jnp.asarray(left_table), jnp.asarray(right_table))
    ))
    return pl.pallas_call(
        finish_kernel,
        out_shape=jax.ShapeDtypeStruct((2, LAGS, TILE, TILE), jnp.float32),
        in_specs=[vmem] * 9,
        out_specs=pl.BlockSpec(memory_space=pltpu.HBM),
        scratch_shapes=[
            pltpu.VMEM((2, LAGS, TILE, TILE), jnp.float32),
            pltpu.VMEM((2, COARSE * TILE, DEPTH), jnp.bfloat16),
            pltpu.VMEM((2, DEPTH, FINE * TILE), jnp.bfloat16),
            dma((COARSE,)),
        ],
        compiler_params=pltpu.CompilerParams(vmem_limit_bytes=12 << 20),
        name="finish",
    )(*rest[:3], partial, *rest[3:])


def lag_tables():
    row = np.arange(DEPTH)
    bin_number = 2 * (row % TILE // PIECE) + row // TILE + 1.0
    angle = np.pi / F * bin_number
    coarse = FINE * np.arange(COARSE) - LAGS // 2
    norm = 1.0 / math.sqrt(F * HOURS)
    left = np.stack([np.cos(coarse[:, None] * angle), np.sin(coarse[:, None] * angle)], axis=1) * norm
    right = np.zeros((DEPTH, TILE))
    for fine in range(1, FINE):
        right[:, 2 * fine - 2] = np.cos(fine * angle)
        right[:, 2 * fine - 1] = np.sin(fine * angle)
    return left.reshape(2 * COARSE, DEPTH).astype(np.float32), right.astype(np.float32)


def per_device(spectra, bad_channels, tile_list):
    rows = spectra.reshape(F * 4, SHARD)
    return fused(rows, bad_channels.reshape(1, SHARD), tile_list.T)


def solution(mesh):
    placed = (P(None, "tm", None, "chan"), P("chan"), P("chan", None))
    return jax.shard_map(
        per_device,
        mesh=mesh,
        in_specs=placed,
        out_specs=P(("chan", "tm"), None, None, None),
        check_vma=False,
    )
```
